512 devices in a mesh: ctx: 128 (over y, z, core), tp: 4 (over x).
Axes of the slice: x: 4, y: 8, z: 8, core: 2. Of those that a mesh axis runs over, the one named last changes fastest.
Arguments:
- streams: bfloat16 [3, 8192, 16384], P(None, 'tp', 'ctx'), may hold values from -6 to 6
- short_weight: float32 [3, 3, 8192], P(None, None, 'tp')
- filters: float32 [512, 16384], P('tp', 'ctx'), may hold values from -0.046875 to 0.046875
- skip_gain: float32 [8192], P('tp'), may hold values from -4 to 4
- norm_gain: float32 [8192], P('tp'), may hold values from 0.5 to 1.5
Outputs:
- block_out: bfloat16 [8192, 16384], P('tp', 'ctx')
The draws below stay inside these ranges and needn't reach their ends.
All inputs are finite; a program needn't handle non-finite values.
Results may differ from the reference program's by a relative error of at most 0.0064.
Values may be sent and summed in bfloat16 or wider, within the bound.
No kernel may reach another device: no remote copies, remote signals or barrier semaphores. Data moves between devices by JAX's collectives and lax.ppermute only.
A program may use at most 64 MiB of HBM per device.

```python
import math
import jax
import jax.numpy as jnp
from jax import lax

GROUPS = 512
C = 8192
SHORT = 3
SEQ = 16384


def draw_short_weight(key, part):
    base = jax.random.normal(key, (SHORT, 3, C), jnp.float32) / math.sqrt(SHORT)
    span = math.log(3.0)
    place = jnp.arange(C).astype(jnp.float32) / (C - 1)
    ramp = jnp.exp(span * place - 0.5 * span)
    scale = jnp.concatenate([ramp[None, :], jnp.ones((2, C), jnp.float32)], axis=0)
    return base * scale[None, :, :]


def level_of(own_key, shape, cuts, smallest, top_value):
    loudness, own = 1.0, jax.random.fold_in(own_key, 6)
    for position, shards_of in cuts:
        heights = jnp.exp(jax.random.uniform(jax.random.fold_in(own, position), (shards_of,), jnp.float32, smallest / len(cuts), top_value / len(cuts)))
        loudness = loudness * jnp.repeat(heights, shape[position] // shards_of).reshape([-1 if axis == position else 1 for axis in range(len(shape))])
    return loudness


def gaussian(stream_key, shape, spread, limit, split=(), kind=jnp.bfloat16):
    level = level_of(stream_key, shape, split, -0.22, 0.18) if split else 1.0
    values = jax.random.normal(stream_key, shape, jnp.float32) * spread * level
    return jnp.minimum(jnp.maximum(values, -limit), limit).astype(kind)


def setup_inputs(seed: int = 0) -> dict:
    splits = jax.random.split(jax.random.key(seed), 6)
    streams = gaussian(splits[0], (3, C, SEQ), 1.0, 6.0, ((1, 4), (2, 128)))
    short_weight = draw_short_weight(jax.random.fold_in(splits[5], 71), 0)
    filters = gaussian(splits[2], (GROUPS, SEQ), SEQ ** -0.5, 0.046875, ((0, 4), (1, 128)), jnp.float32)
    skip_gain = gaussian(splits[3], (C,), 1.0, 4.0, ((0, 4),), jnp.float32)
    norm_gain = jnp.clip(1.0 + 0.1 * jax.random.normal(splits[4], (C,), jnp.float32), 0.5, 1.5)
    return {"streams": streams, "short_weight": short_weight, "filters": filters, "skip_gain": skip_gain, "norm_gain": norm_gain}


def reference(streams, short_weight, filters, skip_gain, norm_gain):
    values = streams.astype(jnp.float32)
    taps = short_weight.shape[0]
    length = values.shape[2]
    padded = jnp.pad(values, ((0, 0), (0, 0), (taps - 1, 0)))
    conv_streams = jnp.zeros(values.shape, jnp.float32)
    for offset in range(taps):
        start = taps - 1 - offset
        conv_streams = conv_streams + short_weight[offset][:, :, None] * padded[:, :, start:start + length]
    query = lax.optimization_barrier(conv_streams[0].astype(jnp.bfloat16)).astype(jnp.float32)
    product = lax.optimization_barrier((conv_streams[1] * conv_streams[2]).astype(jnp.bfloat16)).astype(jnp.float32)
    group_count = filters.shape[0]
    channel_count = product.shape[0]
    grouped = product.reshape(group_count, channel_count // group_count, length)

    def one_group(pair):
        block, taps_row = pair
        spectrum = jnp.fft.rfft(block, n=2 * length, axis=1) * jnp.fft.rfft(taps_row, n=2 * length)[None, :]
        return jnp.fft.irfft(spectrum, n=2 * length, axis=1)[:, :length]
    long_conv = lax.map(one_group, (grouped, filters)).reshape(channel_count, length)
    gated = (query * (long_conv + skip_gain[:, None] * product)).astype(jnp.bfloat16)
    gated_wide = lax.optimization_barrier(gated).astype(jnp.float32)
    rms = jnp.sqrt(lax.optimization_barrier(jnp.mean(gated_wide * gated_wide, axis=0)) + 1e-05)
    return (gated_wide * norm_gain[:, None] / rms[None, :]).astype(jnp.bfloat16)
```

```python
import jax
import jax.numpy as jnp
from jax import lax
from jax.experimental import pallas as pl
from jax.experimental.pallas import tpu as pltpu
from jax.sharding import PartitionSpec as P

bf16 = jnp.bfloat16
f32 = jnp.float32
LANES = 128
SLOT = 24


def long_conv_blocks(recv, owned):
    blocks = recv.shape[0]
    half = blocks // 2
    rows = half * owned
    span = 2
    wide = 2 * LANES

    def kernel(recv_ref, out_ref, toep_ref, cols_ref, acc_ref):
        even = recv_ref[:, 0, 0:owned, :].reshape(rows, LANES)
        odd = recv_ref[:, 1, 0:owned, :].reshape(rows, LANES)
        for lag in range(span):
            skip = lag * owned
            if lag:
                cols_ref[0:skip, lag * wide : (lag + 1) * wide] = jnp.zeros((skip, wide), bf16)
            cols_ref[skip:rows, lag * wide : lag * wide + LANES] = even[0 : rows - skip]
            cols_ref[skip:rows, lag * wide + LANES : (lag + 1) * wide] = odd[0 : rows - skip]
        acc_ref[...] = jnp.zeros_like(acc_ref)
        upper = lax.broadcasted_iota(jnp.int32, (LANES, LANES), 1) >= lax.broadcasted_iota(
            jnp.int32, (LANES, LANES), 0
        )
        toep_ref[0] = jnp.zeros((LANES, LANES), bf16)

        def build(first, count, before):
            for k in range(first, first + count):
                taps = recv_ref[k // 2, k % 2, owned : owned + 8, :].astype(f32)[0:1]
                turned = pltpu.roll(jnp.broadcast_to(taps, (LANES, LANES)), 0, 1, stride=1, stride_axis=0)
                toep_ref[k + 1] = jnp.where(upper, turned, before).astype(bf16)
                before = turned
            return before

        before = build(0, 2 * span, jnp.zeros((LANES, LANES), f32))
        for step in range(half // span):
            if (step + 1) * span < half:
                before = build((step + 1) * 2 * span, 2 * span, before)
            parts = []
            for lag in range(step * span, (step + 1) * span):
                parts.append(jnp.concatenate([toep_ref[2 * lag + 1], toep_ref[2 * lag + 2]], axis=1))
                parts.append(jnp.concatenate([toep_ref[2 * lag], toep_ref[2 * lag + 1]], axis=1))
            start = step * span * owned
            acc_ref[start:rows, :] += jnp.dot(
                cols_ref[0 : rows - start, :], jnp.concatenate(parts, axis=0), preferred_element_type=f32
            )
        out_ref[:, 0] = acc_ref[:, 0:LANES].astype(bf16).reshape(half, owned, LANES)
        out_ref[:, 1] = acc_ref[:, LANES:wide].astype(bf16).reshape(half, owned, LANES)

    out = pl.pallas_call(
        kernel,
        out_shape=jax.ShapeDtypeStruct((half, 2, owned, LANES), bf16),
        in_specs=[pl.BlockSpec(memory_space=pltpu.VMEM)],
        out_specs=pl.BlockSpec(memory_space=pltpu.VMEM),
        scratch_shapes=[
            pltpu.VMEM((blocks + 1, LANES, LANES), bf16),
            pltpu.VMEM((rows, span * wide), bf16),
            pltpu.VMEM((rows, wide), f32),
        ],
        compiler_params=pltpu.CompilerParams(vmem_limit_bytes=32 << 20),
        name="long_conv",
    )(recv.reshape(half, 2, recv.shape[1], LANES))
    return out.reshape(blocks, owned, LANES)


def shards(streams, short_weight, filters, skip_gain, norm_gain):
    n_ctx = lax.axis_size("ctx")
    n_width = lax.axis_size("tp")
    tok_rows = streams.shape[2]
    local_chan = streams.shape[1]
    owned = local_chan // n_ctx
    taps = short_weight.shape[0]
    tail = lax.ppermute(streams[:, :, tok_rows - (taps - 1) :], "ctx", [(i, i + 1) for i in range(n_ctx - 1)])
    padded = jnp.concatenate([tail, streams], axis=2).astype(f32)
    conv = jnp.zeros(streams.shape, f32)
    for offset in range(taps):
        start = taps - 1 - offset
        conv = conv + short_weight[offset][:, :, None] * padded[:, :, start : start + tok_rows]
    query = lax.optimization_barrier(conv[0].astype(bf16))
    product = lax.optimization_barrier((conv[1] * conv[2]).astype(bf16))
    send = jnp.concatenate(
        [
            product.reshape(n_ctx, owned, tok_rows),
            filters.astype(bf16)[:, None, :],
            jnp.zeros((n_ctx, SLOT - owned - 1, tok_rows), bf16),
        ],
        axis=1,
    )
    recv = lax.all_to_all(send, "ctx", 0, 0)
    mixed = long_conv_blocks(recv, owned)
    back = lax.all_to_all(mixed, "ctx", 0, 0).reshape(local_chan, tok_rows)
    gated = (
        query.astype(f32) * (back.astype(f32) + skip_gain[:, None] * product.astype(f32))
    ).astype(bf16)
    gated_wide = lax.optimization_barrier(gated).astype(f32)
    squares = lax.psum(jnp.sum(gated_wide * gated_wide, axis=0), "tp")
    rms = jnp.sqrt(squares / (local_chan * n_width) + 1e-05)
    return (gated_wide * norm_gain[:, None] / rms[None, :]).astype(bf16)


def solution(mesh):
    in_specs = (P(None, "tp", "ctx"), P(None, None, "tp"), P("tp", "ctx"), P("tp"), P("tp"))
    out_specs = P("tp", "ctx")
    return jax.shard_map(shards, mesh=mesh, in_specs=in_specs, out_specs=out_specs, check_vma=False)
```

```python
import jax
import jax.numpy as jnp
import numpy as np
from jax import lax
from jax.experimental import pallas as pl
from jax.experimental.pallas import tpu as pltpu
from jax.sharding import PartitionSpec as P

bf16 = jnp.bfloat16
f32 = jnp.float32
LANES = 128
SLOT = 24


def lane_iota(shape):
    return lax.broadcasted_iota(jnp.int32, shape, len(shape) - 1)


def row_iota(shape):
    return lax.broadcasted_iota(jnp.int32, shape, len(shape) - 2)


ENDS = (0, 1, LANES - 2, LANES - 1)


def pack_product(streams, short_weight, filters, owned):
    chan = streams.shape[1]
    owners = chan // owned
    chunk = 256
    taps = short_weight.shape[0]

    def kernel(key_ref, value_ref, weight_ref, filt_ref, out_ref, ends_ref):
        src = row_iota((LANES, LANES))
        dst = lane_iota((LANES, LANES))
        shifts = jnp.concatenate(
            [jnp.where(dst == src + j, 1.0, 0.0) for j in range(1, taps)], axis=1
        ).astype(bf16)
        place = dst // owned
        pick = []
        for stream in range(2):
            hit = jnp.zeros((LANES, LANES), f32)
            for n, pos in enumerate(ENDS):
                hit = jnp.where((place == 4 * stream + n) & (src == pos), 1.0, hit)
            pick.append(hit)
        pick = jnp.concatenate(pick, axis=0).astype(bf16)
        shape = (chunk, LANES)
        inner = lane_iota(shape) >= taps - 1
        same = lane_iota(shape) % owned == row_iota(shape) % owned
        ends = jnp.zeros((owners, LANES), f32)
        for first in range(0, chan, chunk):
            rows = slice(first, first + chunk)
            columns = jnp.transpose(weight_ref[:, rows])
            key = key_ref[0, rows, :]
            value = value_ref[0, rows, :]
            convs = []
            for stream, raw in ((1, key), (2, value)):
                moved = jnp.dot(raw, shifts, preferred_element_type=f32)
                total = columns[:, stream : stream + 1] * raw.astype(f32)
                for j in range(1, taps):
                    total = total + columns[:, 3 * j + stream : 3 * j + stream + 1] * (
                        moved[:, (j - 1) * LANES : j * LANES]
                    )
                convs.append(total)
            product = jnp.where(inner, convs[0] * convs[1], 0.0).astype(bf16)
            out_ref[first // owned : (first + chunk) // owned, 0:owned, :] = product.reshape(
                chunk // owned, owned, LANES
            )
            spread = jnp.dot(jnp.concatenate([key, value], axis=1), pick, preferred_element_type=f32)
            spread = jnp.where(same, spread, 0.0).astype(bf16)
            group_shape = (owners, chunk)
            member = row_iota(group_shape) == (lane_iota(group_shape) + first) // owned
            ends = ends + jnp.dot(
                jnp.where(member, 1.0, 0.0).astype(bf16), spread, preferred_element_type=f32
            )
        ends_ref[...] = ends
        sub = row_iota((8, LANES))
        for owner in range(owners):
            row = jnp.where(
                sub == 0,
                jnp.broadcast_to(filt_ref[owner : owner + 1, :], (8, LANES)),
                jnp.broadcast_to(ends_ref[owner : owner + 1, :], (8, LANES)),
            )
            out_ref[owner, owned : owned + 8, :] = jnp.where(sub < 2, row, 0.0).astype(bf16)

    weights = jnp.pad(short_weight.reshape(3 * taps, chan), ((0, 16 - 3 * taps), (0, 0)))
    return pl.pallas_call(
        kernel,
        grid=(1,),
        out_shape=jax.ShapeDtypeStruct((owners, SLOT, LANES), bf16),
        in_specs=[
            pl.BlockSpec((1, chan, LANES), lambda i: (1, 0, 0)),
            pl.BlockSpec((1, chan, LANES), lambda i: (2, 0, 0)),
            pl.BlockSpec((16, chan), lambda i: (0, 0)),
            pl.BlockSpec((owners, LANES), lambda i: (0, 0)),
        ],
        out_specs=pl.BlockSpec((owners, SLOT, LANES), lambda i: (0, 0, 0)),
        scratch_shapes=[pltpu.VMEM((owners, LANES), f32)],
        compiler_params=pltpu.CompilerParams(vmem_limit_bytes=32 << 20),
        name="pack_product",
    )(streams, streams, weights, filters)


def end_terms(owned):
    pick = np.zeros((2 * LANES, 6 * LANES), np.float32)
    for stream in range(2):
        base = 4 * stream
        for n, sources in enumerate((((0, 0), (1, 0)), ((3, 1), (0, 0)), ((2, 1), (3, 1)))):
            for pos, (end, before) in enumerate(sources):
                for c in range(owned):
                    row = before * LANES + (base + end) * owned + c
                    pick[row, (3 * stream + n) * LANES + pos * owned + c] = 1.0
    return jnp.asarray(pick, bf16)


def long_conv_blocks(recv, own_weight, owned):
    blocks = recv.shape[0]
    half = blocks // 2
    rows = half * owned
    span = 2
    wide = 2 * LANES
    chunk = 256

    def kernel(recv_ref, weight_ref, terms_ref, out_ref, toep_ref, cols_ref, acc_ref, ends_ref, first_ref):
        for k in range(blocks):
            ends_ref[k : k + 1, :] = recv_ref[k // 2, k % 2, owned : owned + 8, :].astype(f32)[1:2]
        ends = ends_ref[...]
        before = jnp.where(row_iota(ends.shape) == 0, 0.0, pltpu.roll(ends, 1, 0))
        both = jnp.concatenate([ends, before], axis=1).astype(bf16)
        terms = jnp.dot(both, terms_ref[...], preferred_element_type=f32)
        convs = []
        for stream in range(2):
            total = jnp.zeros((blocks, LANES), f32)
            for n in range(3):
                at = 3 * stream + n
                total = total + weight_ref[at : at + 1, :] * terms[:, at * LANES : (at + 1) * LANES]
            convs.append(total)
        first_ref[...] = (convs[0] * convs[1]).astype(bf16)
        shape = (chunk, LANES)
        same = lane_iota(shape) % owned == row_iota(shape) % owned
        src = row_iota((LANES, LANES))
        dst = lane_iota((LANES, LANES))
        to_lane = jnp.where((src // owned == dst) & (dst < 2), 1.0, 0.0).astype(bf16)
        for lag in range(1, span):
            cols_ref[0 : lag * owned, lag * wide : (lag + 1) * wide] = jnp.zeros((lag * owned, wide), bf16)
        for parity in range(2):
            for begin in range(0, rows, chunk):
                block = 2 * ((row_iota(shape) + begin) // owned) + parity
                member = jnp.where(lane_iota(shape) == block, 1.0, 0.0).astype(bf16)
                spread = jnp.dot(member, first_ref[...], preferred_element_type=f32)
                spread = jnp.where(same, spread, 0.0).astype(bf16)
                patch = jnp.dot(spread, to_lane, preferred_element_type=f32)
                part = recv_ref[begin // owned : (begin + chunk) // owned, parity, 0:owned, :]
                part = (part.reshape(chunk, LANES).astype(f32) + patch).astype(bf16)
                for lag in range(span):
                    top = begin + lag * owned
                    size = min(chunk, rows - top)
                    left = lag * wide + parity * LANES
                    cols_ref[top : top + size, left : left + LANES] = part[0:size]
        acc_ref[...] = jnp.zeros_like(acc_ref)
        upper = dst >= src
        toep_ref[0] = jnp.zeros((LANES, LANES), bf16)

        def build(first, count, before):
            for k in range(first, first + count):
                taps = recv_ref[k // 2, k % 2, owned : owned + 8, :].astype(f32)[0:1]
                turned = pltpu.roll(jnp.broadcast_to(taps, (LANES, LANES)), 0, 1, stride=1, stride_axis=0)
                toep_ref[k + 1] = jnp.where(upper, turned, before).astype(bf16)
                before = turned
            return before

        before = build(0, 2 * span, jnp.zeros((LANES, LANES), f32))
        for step in range(half // span):
            if (step + 1) * span < half:
                before = build((step + 1) * 2 * span, 2 * span, before)
            parts = []
            for lag in range(step * span, (step + 1) * span):
                parts.append(jnp.concatenate([toep_ref[2 * lag + 1], toep_ref[2 * lag + 2]], axis=1))
                parts.append(jnp.concatenate([toep_ref[2 * lag], toep_ref[2 * lag + 1]], axis=1))
            start = step * span * owned
            acc_ref[start:rows, :] += jnp.dot(
                cols_ref[0 : rows - start, :], jnp.concatenate(parts, axis=0), preferred_element_type=f32
            )
        out_ref[:, 0] = acc_ref[:, 0:LANES].astype(bf16).reshape(half, owned, LANES)
        out_ref[:, 1] = acc_ref[:, LANES:wide].astype(bf16).reshape(half, owned, LANES)

    vmem = pl.BlockSpec(memory_space=pltpu.VMEM)
    out = pl.pallas_call(
        kernel,
        out_shape=jax.ShapeDtypeStruct((half, 2, owned, LANES), bf16),
        in_specs=[vmem, vmem, vmem],
        out_specs=vmem,
        scratch_shapes=[
            pltpu.VMEM((blocks + 1, LANES, LANES), bf16),
            pltpu.VMEM((rows, span * wide), bf16),
            pltpu.VMEM((rows, wide), f32),
            pltpu.VMEM((blocks, LANES), f32),
            pltpu.VMEM((blocks, LANES), bf16),
        ],
        compiler_params=pltpu.CompilerParams(vmem_limit_bytes=32 << 20),
        name="long_conv",
    )(recv.reshape(half, 2, recv.shape[1], LANES), own_weight, end_terms(owned))
    return out.reshape(blocks, owned, LANES)


def local_streams(streams, short_weight, n_ctx):
    taps = short_weight.shape[0]
    length = streams.shape[2]
    tail = lax.ppermute(streams[:, :, length - (taps - 1) :], "ctx", [(i, i + 1) for i in range(n_ctx - 1)])
    padded = jnp.concatenate([tail, streams], axis=2).astype(f32)
    conv = jnp.zeros(streams.shape, f32)
    for offset in range(taps):
        start = taps - 1 - offset
        conv = conv + short_weight[offset][:, :, None] * padded[:, :, start : start + length]
    return lax.optimization_barrier((conv[0].astype(bf16), (conv[1] * conv[2]).astype(bf16)))


def shards(streams, short_weight, filters, skip_gain, norm_gain):
    n_ctx = lax.axis_size("ctx")
    n_width = lax.axis_size("tp")
    length = streams.shape[2]
    local_chan = streams.shape[1]
    owned = local_chan // n_ctx
    taps = short_weight.shape[0]
    send = pack_product(streams, short_weight, filters, owned)
    recv = lax.all_to_all(send, "ctx", 0, 0)
    streams, short_weight, skip_gain, norm_gain, _ = lax.optimization_barrier(
        (streams, short_weight, skip_gain, norm_gain, send)
    )
    own_weight = lax.dynamic_slice_in_dim(short_weight, lax.axis_index("ctx") * owned, owned, 2)
    own_weight = jnp.transpose(own_weight[:, 1:], (1, 0, 2)).reshape(2 * taps, owned)
    own_weight = jnp.pad(jnp.tile(own_weight, (1, 2)), ((0, 8 - 2 * taps), (0, LANES - 2 * owned)))
    query, product = local_streams(streams, short_weight, n_ctx)
    direct = skip_gain[:, None] * product.astype(f32)
    gain = jnp.broadcast_to(norm_gain[:, None], (local_chan, length))
    direct, gain, own_weight, query, recv = lax.optimization_barrier((direct, gain, own_weight, query, recv))
    mixed = long_conv_blocks(recv, own_weight, owned)
    back = lax.all_to_all(mixed, "ctx", 0, 0).reshape(local_chan, length)
    gated = (query.astype(f32) * (back.astype(f32) + direct)).astype(bf16)
    gated_wide = lax.optimization_barrier(gated).astype(f32)
    squares = jnp.sum(lax.all_gather(jnp.sum(gated_wide * gated_wide, axis=0), "tp"), axis=0)
    rms = jnp.sqrt(squares / (local_chan * n_width) + 1e-05)
    return (gated_wide * gain / rms[None, :]).astype(bf16)


def solution(mesh):
    in_specs = (P(None, "tp", "ctx"), P(None, None, "tp"), P("tp", "ctx"), P("tp"), P("tp"))
    out_specs = P("tp", "ctx")
    return jax.shard_map(shards, mesh=mesh, in_specs=in_specs, out_specs=out_specs, check_vma=False)
```

```python
import jax
import jax.numpy as jnp
import numpy as np
from jax import lax
from jax.experimental import pallas as pl
from jax.experimental.pallas import tpu as pltpu
from jax.sharding import PartitionSpec as P

bf16 = jnp.bfloat16
f32 = jnp.float32
LANES = 128
SLOT = 24


def lane_iota(shape):
    return lax.broadcasted_iota(jnp.int32, shape, len(shape) - 1)


def row_iota(shape):
    return lax.broadcasted_iota(jnp.int32, shape, len(shape) - 2)


ENDS = (0, 1, LANES - 2, LANES - 1)


def pack_product(streams, short_weight, filters, owned):
    chan = streams.shape[1]
    owners = chan // owned
    chunk = 256
    taps = short_weight.shape[0]

    def kernel(key_ref, value_ref, weight_ref, filt_ref, out_ref, ends_ref):
        src = row_iota((LANES, LANES))
        dst = lane_iota((LANES, LANES))
        shifts = jnp.concatenate(
            [jnp.where(dst == src + j, 1.0, 0.0) for j in range(1, taps)], axis=1
        ).astype(bf16)
        place = dst // owned
        pick = []
        for stream in range(2):
            hit = jnp.zeros((LANES, LANES), f32)
            for n, pos in enumerate(ENDS):
                hit = jnp.where((place == 4 * stream + n) & (src == pos), 1.0, hit)
            pick.append(hit)
        pick = jnp.concatenate(pick, axis=0).astype(bf16)
        shape = (chunk, LANES)
        inner = lane_iota(shape) >= taps - 1
        same = lane_iota(shape) % owned == row_iota(shape) % owned
        ends = jnp.zeros((owners, LANES), f32)
        for first in range(0, chan, chunk):
            rows = slice(first, first + chunk)
            columns = jnp.transpose(weight_ref[:, rows])
            key = key_ref[0, rows, :]
            value = value_ref[0, rows, :]
            convs = []
            for stream, raw in ((1, key), (2, value)):
                moved = jnp.dot(raw, shifts, preferred_element_type=f32)
                total = columns[:, stream : stream + 1] * raw.astype(f32)
                for j in range(1, taps):
                    total = total + columns[:, 3 * j + stream : 3 * j + stream + 1] * (
                        moved[:, (j - 1) * LANES : j * LANES]
                    )
                convs.append(total)
            product = jnp.where(inner, convs[0] * convs[1], 0.0).astype(bf16)
            out_ref[first // owned : (first + chunk) // owned, 0:owned, :] = product.reshape(
                chunk // owned, owned, LANES
            )
            spread = jnp.dot(jnp.concatenate([key, value], axis=1), pick, preferred_element_type=f32)
            spread = jnp.where(same, spread, 0.0).astype(bf16)
            group_shape = (owners, chunk)
            member = row_iota(group_shape) == (lane_iota(group_shape) + first) // owned
            ends = ends + jnp.dot(
                jnp.where(member, 1.0, 0.0).astype(bf16), spread, preferred_element_type=f32
            )
        ends_ref[...] = ends
        sub = row_iota((8, LANES))
        for owner in range(owners):
            row = jnp.where(
                sub == 0,
                jnp.broadcast_to(filt_ref[owner : owner + 1, :], (8, LANES)),
                jnp.broadcast_to(ends_ref[owner : owner + 1, :], (8, LANES)),
            )
            out_ref[owner, owned : owned + 8, :] = jnp.where(sub < 2, row, 0.0).astype(bf16)

    weights = jnp.pad(short_weight.reshape(3 * taps, chan), ((0, 16 - 3 * taps), (0, 0)))
    return pl.pallas_call(
        kernel,
        grid=(1,),
        out_shape=jax.ShapeDtypeStruct((owners, SLOT, LANES), bf16),
        in_specs=[
            pl.BlockSpec((1, chan, LANES), lambda i: (1, 0, 0)),
            pl.BlockSpec((1, chan, LANES), lambda i: (2, 0, 0)),
            pl.BlockSpec((16, chan), lambda i: (0, 0)),
            pl.BlockSpec((owners, LANES), lambda i: (0, 0)),
        ],
        out_specs=pl.BlockSpec((owners, SLOT, LANES), lambda i: (0, 0, 0)),
        scratch_shapes=[pltpu.VMEM((owners, LANES), f32)],
        compiler_params=pltpu.CompilerParams(vmem_limit_bytes=32 << 20),
        name="pack_product",
    )(streams, streams, weights, filters)


def end_terms(owned):
    pick = np.zeros((2 * LANES, 6 * LANES), np.float32)
    for stream in range(2):
        base = 4 * stream
        for n, sources in enumerate((((0, 0), (1, 0)), ((3, 1), (0, 0)), ((2, 1), (3, 1)))):
            for pos, (end, before) in enumerate(sources):
                for c in range(owned):
                    row = before * LANES + (base + end) * owned + c
                    pick[row, (3 * stream + n) * LANES + pos * owned + c] = 1.0
    return jnp.asarray(pick, bf16)


def long_conv_blocks(recv, own_weight, owned):
    blocks = recv.shape[0]
    half = blocks // 2
    rows = half * owned
    span = 2
    wide = 2 * LANES
    chunk = 256

    def kernel(recv_ref, weight_ref, terms_ref, out_ref, toep_ref, cols_ref, acc_ref, ends_ref, first_ref):
        for k in range(blocks):
            ends_ref[k : k + 1, :] = recv_ref[k // 2, k % 2, owned : owned + 8, :].astype(f32)[1:2]
        ends = ends_ref[...]
        before = jnp.where(row_iota(ends.shape) == 0, 0.0, pltpu.roll(ends, 1, 0))
        both = jnp.concatenate([ends, before], axis=1).astype(bf16)
        terms = jnp.dot(both, terms_ref[...], preferred_element_type=f32)
        convs = []
        for stream in range(2):
            total = jnp.zeros((blocks, LANES), f32)
            for n in range(3):
                at = 3 * stream + n
                total = total + weight_ref[at : at + 1, :] * terms[:, at * LANES : (at + 1) * LANES]
            convs.append(total)
        first_ref[...] = (convs[0] * convs[1]).astype(bf16)
        shape = (chunk, LANES)
        same = lane_iota(shape) % owned == row_iota(shape) % owned
        src = row_iota((LANES, LANES))
        dst = lane_iota((LANES, LANES))
        to_lane = jnp.where((src // owned == dst) & (dst < 2), 1.0, 0.0).astype(bf16)
        for lag in range(1, span):
            cols_ref[0 : lag * owned, lag * wide : (lag + 1) * wide] = jnp.zeros((lag * owned, wide), bf16)
        for parity in range(2):
            for begin in range(0, rows, chunk):
                block = 2 * ((row_iota(shape) + begin) // owned) + parity
                member = jnp.where(lane_iota(shape) == block, 1.0, 0.0).astype(bf16)
                spread = jnp.dot(member, first_ref[...], preferred_element_type=f32)
                spread = jnp.where(same, spread, 0.0).astype(bf16)
                patch = jnp.dot(spread, to_lane, preferred_element_type=f32)
                part = recv_ref[begin // owned : (begin + chunk) // owned, parity, 0:owned, :]
                part = (part.reshape(chunk, LANES).astype(f32) + patch).astype(bf16)
                for lag in range(span):
                    top = begin + lag * owned
                    size = min(chunk, rows - top)
                    left = lag * wide + parity * LANES
                    cols_ref[top : top + size, left : left + LANES] = part[0:size]
        acc_ref[...] = jnp.zeros_like(acc_ref)
        upper = dst >= src
        toep_ref[0] = jnp.zeros((LANES, LANES), bf16)

        def build(first, count, before):
            for k in range(first, first + count):
                taps = recv_ref[k // 2, k % 2, owned : owned + 8, :].astype(f32)[0:1]
                turned = pltpu.roll(jnp.broadcast_to(taps, (LANES, LANES)), 0, 1, stride=1, stride_axis=0)
                toep_ref[k + 1] = jnp.where(upper, turned, before).astype(bf16)
                before = turned
            return before

        before = build(0, 2 * span, jnp.zeros((LANES, LANES), f32))
        for step in range(half // span):
            if (step + 1) * span < half:
                before = build((step + 1) * 2 * span, 2 * span, before)
            parts = []
            for lag in range(step * span, (step + 1) * span):
                parts.append(jnp.concatenate([toep_ref[2 * lag + 1], toep_ref[2 * lag + 2]], axis=1))
                parts.append(jnp.concatenate([toep_ref[2 * lag], toep_ref[2 * lag + 1]], axis=1))
            start = step * span * owned
            acc_ref[start:rows, :] += jnp.dot(
                cols_ref[0 : rows - start, :], jnp.concatenate(parts, axis=0), preferred_element_type=f32
            )
        out_ref[:, 0] = acc_ref[:, 0:LANES].astype(bf16).reshape(half, owned, LANES)
        out_ref[:, 1] = acc_ref[:, LANES:wide].astype(bf16).reshape(half, owned, LANES)

    vmem = pl.BlockSpec(memory_space=pltpu.VMEM)
    out = pl.pallas_call(
        kernel,
        out_shape=jax.ShapeDtypeStruct((half, 2, owned, LANES), bf16),
        in_specs=[vmem, vmem, vmem],
        out_specs=vmem,
        scratch_shapes=[
            pltpu.VMEM((blocks + 1, LANES, LANES), bf16),
            pltpu.VMEM((rows, span * wide), bf16),
            pltpu.VMEM((rows, wide), f32),
            pltpu.VMEM((blocks, LANES), f32),
            pltpu.VMEM((blocks, LANES), bf16),
        ],
        compiler_params=pltpu.CompilerParams(vmem_limit_bytes=32 << 20),
        name="long_conv",
    )(recv.reshape(half, 2, recv.shape[1], LANES), own_weight, end_terms(owned))
    return out.reshape(blocks, owned, LANES)


def local_streams(streams, tail, short_weight):
    taps = short_weight.shape[0]
    length = streams.shape[2]
    padded = jnp.concatenate([tail, streams], axis=2).astype(f32)
    conv = jnp.zeros(streams.shape, f32)
    for offset in range(taps):
        start = taps - 1 - offset
        conv = conv + short_weight[offset][:, :, None] * padded[:, :, start : start + length]
    return lax.optimization_barrier((conv[0].astype(bf16), (conv[1] * conv[2]).astype(bf16)))


def shards(streams, short_weight, filters, skip_gain, norm_gain):
    n_ctx = lax.axis_size("ctx")
    n_width = lax.axis_size("tp")
    length = streams.shape[2]
    local_chan = streams.shape[1]
    owned = local_chan // n_ctx
    taps = short_weight.shape[0]
    send = pack_product(streams, short_weight, filters, owned)
    recv = lax.all_to_all(send, "ctx", 0, 0)
    streams, short_weight, _ = lax.optimization_barrier((streams, short_weight, send))
    own_weight = lax.dynamic_slice_in_dim(short_weight, lax.axis_index("ctx") * owned, owned, 2)
    own_weight = jnp.transpose(own_weight[:, 1:], (1, 0, 2)).reshape(2 * taps, owned)
    own_weight = jnp.pad(jnp.tile(own_weight, (1, 2)), ((0, 8 - 2 * taps), (0, LANES - 2 * owned)))
    tail = lax.ppermute(streams[:, :, length - (taps - 1) :], "ctx", [(i, i + 1) for i in range(n_ctx - 1)])
    mixed = long_conv_blocks(recv, own_weight, owned)
    back = lax.all_to_all(mixed, "ctx", 0, 0).reshape(local_chan, length)
    streams, tail, short_weight, skip_gain, norm_gain, _ = lax.optimization_barrier(
        (streams, tail, short_weight, skip_gain, norm_gain, mixed)
    )
    query, product = local_streams(streams, tail, short_weight)
    direct = skip_gain[:, None] * product.astype(f32)
    gain = jnp.broadcast_to(norm_gain[:, None], (local_chan, length))
    direct, gain, query, back = lax.optimization_barrier((direct, gain, query, back))
    gated = (query.astype(f32) * (back.astype(f32) + direct)).astype(bf16)
    gated_wide = lax.optimization_barrier(gated).astype(f32)
    squares = jnp.sum(lax.all_gather(jnp.sum(gated_wide * gated_wide, axis=0), "tp"), axis=0)
    rms = jnp.sqrt(squares / (local_chan * n_width) + 1e-05)
    return (gated_wide * gain / rms[None, :]).astype(bf16)


def solution(mesh):
    in_specs = (P(None, "tp", "ctx"), P(None, None, "tp"), P("tp", "ctx"), P("tp"), P("tp"))
    out_specs = P("tp", "ctx")
    return jax.shard_map(shards, mesh=mesh, in_specs=in_specs, out_specs=out_specs, check_vma=False)
```

```python
import jax
import jax.numpy as jnp
import numpy as np
from jax import lax
from jax.experimental import pallas as pl
from jax.experimental.pallas import tpu as pltpu
from jax.sharding import PartitionSpec as P

bf16 = jnp.bfloat16
f32 = jnp.float32
LANES = 128


def lane_iota(shape):
    return lax.broadcasted_iota(jnp.int32, shape, len(shape) - 1)


def row_iota(shape):
    return lax.broadcasted_iota(jnp.int32, shape, len(shape) - 2)


ENDS = (0, 1, LANES - 2, LANES - 1)


def pack_product(streams, short_weight, filters, owned):
    taps, _, chan = short_weight.shape
    owners = chan // owned
    chunk = 1024
    per = chunk // owned
    terms = 2 * taps

    def kernel(key_ref, value_ref, weight_ref, filt_ref, out_ref):
        src = row_iota((LANES, LANES))
        place = lane_iota((LANES, LANES)) // owned
        pick = []
        for stream in range(2):
            hit = jnp.zeros((LANES, LANES), f32)
            for n, pos in enumerate(ENDS):
                hit = jnp.where((place == 4 * stream + n) & (src == pos), 1.0, hit)
            pick.append(hit)
        pick = jnp.concatenate(pick, axis=0).astype(bf16)
        weight = weight_ref[...].reshape(3 * taps, chunk)
        high = weight.astype(bf16).astype(f32)
        middle = (weight - high).astype(bf16).astype(f32)
        parts = [high, middle, weight - high - middle, jnp.zeros((32 - 9 * taps, chunk), f32)]
        parts = jnp.transpose(jnp.concatenate(parts, axis=0)).astype(bf16)
        row = row_iota((32, terms * LANES))
        block = lane_iota((32, terms * LANES)) // LANES
        wanted = 3 * (block % taps) + block // taps + 1
        choose = jnp.where((row % (3 * taps) == wanted) & (row < 9 * taps), 1.0, 0.0).astype(bf16)
        along = jnp.dot(parts, choose, preferred_element_type=f32)
        shape = (chunk, LANES)
        convs = []
        for stream, raw_ref in enumerate((key_ref, value_ref)):
            raw = raw_ref[0].astype(f32)
            total = along[:, stream * taps * LANES : (stream * taps + 1) * LANES] * raw
            for j in range(1, taps):
                at = (stream * taps + j) * LANES
                total = total + along[:, at : at + LANES] * pltpu.roll(raw, j, 1)
            convs.append(total)
        product = jnp.where(lane_iota(shape) >= taps - 1, convs[0] * convs[1], 0.0).astype(bf16)
        out_ref[:, 0 : owned // 2] = product.reshape(per, owned // 2, 2, LANES)
        same = lane_iota(shape) % owned == row_iota(shape) % owned
        spread = jnp.dot(
            jnp.concatenate([key_ref[0], value_ref[0]], axis=1), pick, preferred_element_type=f32
        )
        spread = jnp.where(same, spread, 0.0).astype(bf16)
        member = row_iota((per, chunk)) == lane_iota((per, chunk)) // owned
        ends = jnp.dot(jnp.where(member, 1.0, 0.0).astype(bf16), spread, preferred_element_type=f32)
        first = row_iota((per, 2, LANES)) == 0
        rest = jnp.where(first, filt_ref[...][:, None, :], ends[:, None, :])
        out_ref[:, owned // 2] = rest.astype(bf16)

    return pl.pallas_call(
        kernel,
        grid=(chan // chunk,),
        out_shape=jax.ShapeDtypeStruct((owners, owned // 2 + 1, 2, LANES), bf16),
        in_specs=[
            pl.BlockSpec((1, chunk, LANES), lambda i: (1, i, 0)),
            pl.BlockSpec((1, chunk, LANES), lambda i: (2, i, 0)),
            pl.BlockSpec((taps, 3, chunk), lambda i: (0, 0, i)),
            pl.BlockSpec((per, LANES), lambda i: (i, 0)),
        ],
        out_specs=pl.BlockSpec((per, owned // 2 + 1, 2, LANES), lambda i: (i, 0, 0, 0)),
        compiler_params=pltpu.CompilerParams(vmem_limit_bytes=32 << 20),
        name="pack_product",
    )(*(pltpu.with_memory_space_constraint(x, pltpu.HBM) for x in (streams, streams, short_weight, filters)))


def end_terms(owned):
    pick = np.zeros((2 * LANES, 6 * LANES), np.float32)
    for stream in range(2):
        base = 4 * stream
        for n, sources in enumerate((((0, 0), (1, 0)), ((3, 1), (0, 0)), ((2, 1), (3, 1)))):
            for pos, (end, before) in enumerate(sources):
                for c in range(owned):
                    row = before * LANES + (base + end) * owned + c
                    pick[row, (3 * stream + n) * LANES + pos * owned + c] = 1.0
    return jnp.asarray(pick, bf16)


def long_conv_blocks(recv, own_weight, owned):
    blocks = recv.shape[0]
    half = blocks // 2
    rows = half * owned
    span = 2
    wide = 2 * LANES
    chunk = 256

    def kernel(recv_ref, weight_ref, terms_ref, out_ref, toep_ref, cols_ref, acc_ref, ends_ref, first_ref):
        for k in range(blocks):
            ends_ref[k : k + 1, :] = recv_ref[k // 2, k % 2, owned // 2].astype(f32)[1:2]
        ends = ends_ref[...]
        before = jnp.where(row_iota(ends.shape) == 0, 0.0, pltpu.roll(ends, 1, 0))
        both = jnp.concatenate([ends, before], axis=1).astype(bf16)
        terms = jnp.dot(both, terms_ref[...], preferred_element_type=f32)
        convs = []
        for stream in range(2):
            total = jnp.zeros((blocks, LANES), f32)
            for n in range(3):
                at = 3 * stream + n
                total = total + weight_ref[at : at + 1, :] * terms[:, at * LANES : (at + 1) * LANES]
            convs.append(total)
        first_ref[...] = (convs[0] * convs[1]).astype(bf16)
        shape = (chunk, LANES)
        same = lane_iota(shape) % owned == row_iota(shape) % owned
        src = row_iota((LANES, LANES))
        dst = lane_iota((LANES, LANES))
        to_lane = jnp.where((src // owned == dst) & (dst < 2), 1.0, 0.0).astype(bf16)
        for lag in range(1, span):
            cols_ref[0 : lag * owned, lag * wide : (lag + 1) * wide] = jnp.zeros((lag * owned, wide), bf16)
        for parity in range(2):
            for begin in range(0, rows, chunk):
                block = 2 * ((row_iota(shape) + begin) // owned) + parity
                member = jnp.where(lane_iota(shape) == block, 1.0, 0.0).astype(bf16)
                spread = jnp.dot(member, first_ref[...], preferred_element_type=f32)
                spread = jnp.where(same, spread, 0.0).astype(bf16)
                patch = jnp.dot(spread, to_lane, preferred_element_type=f32)
                part = recv_ref[begin // owned : (begin + chunk) // owned, parity, 0 : owned // 2]
                part = (part.reshape(chunk, LANES).astype(f32) + patch).astype(bf16)
                for lag in range(span):
                    top = begin + lag * owned
                    size = min(chunk, rows - top)
                    left = lag * wide + parity * LANES
                    cols_ref[top : top + size, left : left + LANES] = part[0:size]
        acc_ref[...] = jnp.zeros_like(acc_ref)
        upper = dst >= src
        toep_ref[0] = jnp.zeros((LANES, LANES), bf16)

        def build(first, count, before):
            for k in range(first, first + count):
                taps = recv_ref[k // 2, k % 2, owned // 2].astype(f32)[0:1]
                turned = pltpu.roll(jnp.broadcast_to(taps, (LANES, LANES)), 0, 1, stride=1, stride_axis=0)
                toep_ref[k + 1] = jnp.where(upper, turned, before).astype(bf16)
                before = turned
            return before

        before = build(0, 2 * span, jnp.zeros((LANES, LANES), f32))
        for step in range(half // span):
            if (step + 1) * span < half:
                before = build((step + 1) * 2 * span, 2 * span, before)
            parts = []
            for lag in range(step * span, (step + 1) * span):
                parts.append(jnp.concatenate([toep_ref[2 * lag + 1], toep_ref[2 * lag + 2]], axis=1))
                parts.append(jnp.concatenate([toep_ref[2 * lag], toep_ref[2 * lag + 1]], axis=1))
            start = step * span * owned
            acc_ref[start:rows, :] += jnp.dot(
                cols_ref[0 : rows - start, :], jnp.concatenate(parts, axis=0), preferred_element_type=f32
            )
        out_ref[:, 0] = acc_ref[:, 0:LANES].astype(bf16).reshape(half, owned, LANES)
        out_ref[:, 1] = acc_ref[:, LANES:wide].astype(bf16).reshape(half, owned, LANES)

    vmem = pl.BlockSpec(memory_space=pltpu.VMEM)
    out = pl.pallas_call(
        kernel,
        out_shape=jax.ShapeDtypeStruct((half, 2, owned, LANES), bf16),
        in_specs=[vmem, vmem, vmem],
        out_specs=vmem,
        scratch_shapes=[
            pltpu.VMEM((blocks + 1, LANES, LANES), bf16),
            pltpu.VMEM((rows, span * wide), bf16),
            pltpu.VMEM((rows, wide), f32),
            pltpu.VMEM((blocks, LANES), f32),
            pltpu.VMEM((blocks, LANES), bf16),
        ],
        compiler_params=pltpu.CompilerParams(vmem_limit_bytes=32 << 20),
        name="long_conv",
    )(recv.reshape((half, 2) + recv.shape[1:]), own_weight, end_terms(owned))
    return out.reshape(blocks, owned, LANES)


def local_streams(streams, tail, short_weight):
    taps = short_weight.shape[0]
    length = streams.shape[2]
    padded = jnp.concatenate([tail, streams], axis=2).astype(f32)
    conv = jnp.zeros(streams.shape, f32)
    for offset in range(taps):
        start = taps - 1 - offset
        conv = conv + short_weight[offset][:, :, None] * padded[:, :, start : start + length]
    return lax.optimization_barrier((conv[0].astype(bf16), (conv[1] * conv[2]).astype(bf16)))


def in_vmem(*arrays):
    return tuple(pltpu.with_memory_space_constraint(x, pltpu.VMEM) for x in arrays)


def gate(back, query, direct, gain):
    chan, length = query.shape
    chunk = chan // 4

    def kernel(back_ref, query_ref, direct_ref, gain_ref, out_ref, sum_ref):
        total = jnp.zeros((8, length), f32)
        for first in range(0, chan, chunk):
            rows = slice(first, first + chunk)
            mixed = back_ref[rows, :].astype(f32) + direct_ref[rows, :]
            gated = (query_ref[rows, :].astype(f32) * mixed).astype(bf16).astype(f32)
            out_ref[rows, :] = gated * gain_ref[rows, :]
            total = total + jnp.sum((gated * gated).reshape(chunk // 8, 8, length), axis=0)
        sum_ref[...] = jnp.sum(total, axis=0, keepdims=True)

    whole = pl.BlockSpec(memory_space=pltpu.VMEM)
    return pl.pallas_call(
        kernel,
        out_shape=(pltpu.VMEM((chan, length), f32), pltpu.VMEM((1, length), f32)),
        in_specs=[whole] * 4,
        out_specs=(whole, whole),
        compiler_params=pltpu.CompilerParams(vmem_limit_bytes=16 << 20),
        name="gate",
    )(*in_vmem(back, query, direct, gain))


def finish(gated, squares, count):
    chan, length = gated.shape

    def kernel(gated_ref, squares_ref, out_ref):
        rms = jnp.sqrt(jnp.sum(squares_ref[...], axis=0) / count + 1e-05)
        out_ref[...] = (gated_ref[...] * (1.0 / rms)).astype(bf16)

    whole = pl.BlockSpec(memory_space=pltpu.VMEM)
    return pl.pallas_call(
        kernel,
        out_shape=jax.ShapeDtypeStruct((chan, length), bf16),
        in_specs=[whole, whole],
        out_specs=whole,
        compiler_params=pltpu.CompilerParams(vmem_limit_bytes=16 << 20),
        name="finish",
    )(*in_vmem(gated), squares)


def shards(streams, short_weight, filters, skip_gain, norm_gain):
    n_ctx = lax.axis_size("ctx")
    n_width = lax.axis_size("tp")
    length = streams.shape[2]
    local_chan = streams.shape[1]
    owned = local_chan // n_ctx
    taps = short_weight.shape[0]
    send = pack_product(streams, short_weight, filters, owned)
    recv = lax.all_to_all(send, "ctx", 0, 0)
    streams, short_weight, _ = lax.optimization_barrier((streams, short_weight, send))
    own_weight = lax.dynamic_slice_in_dim(short_weight, lax.axis_index("ctx") * owned, owned, 2)
    own_weight = jnp.transpose(own_weight[:, 1:], (1, 0, 2)).reshape(2 * taps, owned)
    own_weight = jnp.pad(jnp.tile(own_weight, (1, 2)), ((0, 8 - 2 * taps), (0, LANES - 2 * owned)))
    tail = lax.ppermute(streams[:, :, length - (taps - 1) :], "ctx", [(i, i + 1) for i in range(n_ctx - 1)])
    mixed = long_conv_blocks(recv, own_weight, owned)
    back = lax.all_to_all(mixed, "ctx", 0, 0).reshape(local_chan, length)
    streams, tail, short_weight, skip_gain, norm_gain, _ = lax.optimization_barrier(
        (streams, tail, short_weight, skip_gain, norm_gain, mixed)
    )
    query, product = local_streams(streams, tail, short_weight)
    gain = jnp.broadcast_to(norm_gain[:, None], (local_chan, length))
    gain, product = lax.optimization_barrier((gain, product))
    direct = skip_gain[:, None] * product.astype(f32)
    direct, gain, query, back = lax.optimization_barrier((direct, gain, query, back))
    gated, squares = gate(back, query, direct, gain)
    return finish(gated, lax.all_gather(squares, "tp"), local_chan * n_width)


def solution(mesh):
    in_specs = (P(None, "tp", "ctx"), P(None, None, "tp"), P("tp", "ctx"), P("tp"), P("tp"))
    out_specs = P("tp", "ctx")
    return jax.shard_map(shards, mesh=mesh, in_specs=in_specs, out_specs=out_specs, check_vma=False)
```

```python
import jax
import jax.numpy as jnp
import numpy as np
from jax import lax
from jax.experimental import pallas as pl
from jax.experimental.pallas import tpu as pltpu
from jax.sharding import PartitionSpec as P

bf16 = jnp.bfloat16
f32 = jnp.float32
LANES = 128


def lane_iota(shape):
    return lax.broadcasted_iota(jnp.int32, shape, len(shape) - 1)


def row_iota(shape):
    return lax.broadcasted_iota(jnp.int32, shape, len(shape) - 2)


ENDS = (0, 1, LANES - 2, LANES - 1)


def pack_product(streams, short_weight, filters, owned):
    taps, _, chan = short_weight.shape
    owners = chan // owned
    chunk = 1024
    per = chunk // owned
    terms = 2 * taps

    def kernel(key_ref, value_ref, weight_ref, filt_ref, out_ref):
        src = row_iota((LANES, LANES))
        place = lane_iota((LANES, LANES)) // owned
        pick = []
        for stream in range(2):
            hit = jnp.zeros((LANES, LANES), f32)
            for n, pos in enumerate(ENDS):
                hit = jnp.where((place == 4 * stream + n) & (src == pos), 1.0, hit)
            pick.append(hit)
        pick = jnp.concatenate(pick, axis=0).astype(bf16)
        weight = weight_ref[...].reshape(3 * taps, chunk)
        high = weight.astype(bf16).astype(f32)
        middle = (weight - high).astype(bf16).astype(f32)
        parts = [high, middle, weight - high - middle, jnp.zeros((32 - 9 * taps, chunk), f32)]
        parts = jnp.transpose(jnp.concatenate(parts, axis=0)).astype(bf16)
        row = row_iota((32, terms * LANES))
        block = lane_iota((32, terms * LANES)) // LANES
        wanted = 3 * (block % taps) + block // taps + 1
        choose = jnp.where((row % (3 * taps) == wanted) & (row < 9 * taps), 1.0, 0.0).astype(bf16)
        along = jnp.dot(parts, choose, preferred_element_type=f32)
        part = chunk // 2
        shape = (part, LANES)
        inner = lane_iota(shape) >= taps - 1
        same = lane_iota(shape) % owned == row_iota(shape) % owned
        for begin in range(0, chunk, part):
            rows = slice(begin, begin + part)
            own = slice(begin // owned, (begin + part) // owned)
            along = jnp.dot(parts[rows], choose, preferred_element_type=f32)
            convs = []
            for stream, raw_ref in enumerate((key_ref, value_ref)):
                raw = raw_ref[0, rows]
                total = along[:, stream * taps * LANES : (stream * taps + 1) * LANES] * raw.astype(f32)
                for j in range(1, taps):
                    at = (stream * taps + j) * LANES
                    total = total + along[:, at : at + LANES] * pltpu.roll(raw, j, 1).astype(f32)
                convs.append(total)
            product = jnp.where(inner, convs[0] * convs[1], 0.0).astype(bf16)
            out_ref[own, 0 : owned // 2] = product.reshape(part // owned, owned // 2, 2, LANES)
            both = jnp.concatenate([key_ref[0, rows], value_ref[0, rows]], axis=1)
            spread = jnp.where(same, jnp.dot(both, pick, preferred_element_type=f32), 0.0)
            ends = jnp.sum(spread.reshape(part // owned, owned, LANES), axis=1)
            first = row_iota((part // owned, 2, LANES)) == 0
            rest = jnp.where(first, filt_ref[own][:, None, :], ends[:, None, :])
            out_ref[own, owned // 2] = rest.astype(bf16)

    return pl.pallas_call(
        kernel,
        grid=(chan // chunk,),
        out_shape=jax.ShapeDtypeStruct((owners, owned // 2 + 1, 2, LANES), bf16),
        in_specs=[
            pl.BlockSpec((1, chunk, LANES), lambda i: (1, i, 0)),
            pl.BlockSpec((1, chunk, LANES), lambda i: (2, i, 0)),
            pl.BlockSpec((taps, 3, chunk), lambda i: (0, 0, i)),
            pl.BlockSpec((per, LANES), lambda i: (i, 0)),
        ],
        out_specs=pl.BlockSpec((per, owned // 2 + 1, 2, LANES), lambda i: (i, 0, 0, 0)),
        compiler_params=pltpu.CompilerParams(vmem_limit_bytes=32 << 20),
        name="pack_product",
    )(*(pltpu.with_memory_space_constraint(x, pltpu.HBM) for x in (streams, streams, short_weight, filters)))


def end_terms(owned):
    pick = np.zeros((2 * LANES, 6 * LANES), np.float32)
    for stream in range(2):
        base = 4 * stream
        for n, sources in enumerate((((0, 0), (1, 0)), ((3, 1), (0, 0)), ((2, 1), (3, 1)))):
            for pos, (end, before) in enumerate(sources):
                for c in range(owned):
                    row = before * LANES + (base + end) * owned + c
                    pick[row, (3 * stream + n) * LANES + pos * owned + c] = 1.0
    return jnp.asarray(pick, bf16)


def long_conv_blocks(recv, own_weight, owned):
    blocks = recv.shape[0]
    half = blocks // 2
    rows = half * owned
    span = 2
    wide = 2 * LANES
    chunk = 256

    def kernel(recv_ref, weight_ref, terms_ref, out_ref, toep_ref, cols_ref, acc_ref, ends_ref, first_ref):
        for k in range(blocks):
            ends_ref[k : k + 1, :] = recv_ref[k // 2, k % 2, owned // 2].astype(f32)[1:2]
        ends = ends_ref[...]
        before = jnp.where(row_iota(ends.shape) == 0, 0.0, pltpu.roll(ends, 1, 0))
        both = jnp.concatenate([ends, before], axis=1).astype(bf16)
        terms = jnp.dot(both, terms_ref[...], preferred_element_type=f32)
        convs = []
        for stream in range(2):
            total = jnp.zeros((blocks, LANES), f32)
            for n in range(3):
                at = 3 * stream + n
                total = total + weight_ref[at : at + 1, :] * terms[:, at * LANES : (at + 1) * LANES]
            convs.append(total)
        first_ref[...] = (convs[0] * convs[1]).astype(bf16).astype(f32)
        shape = (owned, LANES)
        same = lane_iota(shape) % owned == row_iota(shape)
        src = row_iota((LANES, LANES))
        dst = lane_iota((LANES, LANES))
        to_lane = jnp.where((src // owned == dst) & (dst < 2), 1.0, 0.0).astype(bf16)
        for lag in range(1, span):
            cols_ref[0 : lag * owned, lag * wide : (lag + 1) * wide] = jnp.zeros((lag * owned, wide), bf16)
        for parity in range(2):
            for begin in range(0, rows, chunk):
                spread = []
                for pair in range(begin // owned, (begin + chunk) // owned):
                    block = 2 * pair + parity
                    values = jnp.broadcast_to(first_ref[block : block + 1, :], shape)
                    spread.append(jnp.where(same, values, 0.0))
                spread = jnp.concatenate(spread, axis=0).astype(bf16)
                patch = jnp.dot(spread, to_lane, preferred_element_type=f32)
                part = recv_ref[begin // owned : (begin + chunk) // owned, parity, 0 : owned // 2]
                part = (part.reshape(chunk, LANES).astype(f32) + patch).astype(bf16)
                for lag in range(span):
                    top = begin + lag * owned
                    size = min(chunk, rows - top)
                    left = lag * wide + parity * LANES
                    cols_ref[top : top + size, left : left + LANES] = part[0:size]
        acc_ref[...] = jnp.zeros_like(acc_ref)
        upper = dst >= src
        toep_ref[0] = jnp.zeros((LANES, LANES), bf16)

        def build(first, count, before):
            for k in range(first, first + count):
                taps = recv_ref[k // 2, k % 2, owned // 2].astype(f32)[0:1]
                turned = pltpu.roll(jnp.broadcast_to(taps, (LANES, LANES)), 0, 1, stride=1, stride_axis=0)
                toep_ref[k + 1] = jnp.where(upper, turned, before).astype(bf16)
                before = turned
            return before

        before = build(0, 2 * span, jnp.zeros((LANES, LANES), f32))
        for step in range(half // span):
            if (step + 1) * span < half:
                before = build((step + 1) * 2 * span, 2 * span, before)
            parts = []
            for lag in range(step * span, (step + 1) * span):
                parts.append(jnp.concatenate([toep_ref[2 * lag + 1], toep_ref[2 * lag + 2]], axis=1))
                parts.append(jnp.concatenate([toep_ref[2 * lag], toep_ref[2 * lag + 1]], axis=1))
            start = step * span * owned
            acc_ref[start:rows, :] += jnp.dot(
                cols_ref[0 : rows - start, :], jnp.concatenate(parts, axis=0), preferred_element_type=f32
            )
        out_ref[:, 0] = acc_ref[:, 0:LANES].astype(bf16).reshape(half, owned, LANES)
        out_ref[:, 1] = acc_ref[:, LANES:wide].astype(bf16).reshape(half, owned, LANES)

    vmem = pl.BlockSpec(memory_space=pltpu.VMEM)
    out = pl.pallas_call(
        kernel,
        out_shape=jax.ShapeDtypeStruct((half, 2, owned, LANES), bf16),
        in_specs=[vmem, vmem, vmem],
        out_specs=vmem,
        scratch_shapes=[
            pltpu.VMEM((blocks + 1, LANES, LANES), bf16),
            pltpu.VMEM((rows, span * wide), bf16),
            pltpu.VMEM((rows, wide), f32),
            pltpu.VMEM((blocks, LANES), f32),
            pltpu.VMEM((blocks, LANES), f32),
        ],
        compiler_params=pltpu.CompilerParams(vmem_limit_bytes=32 << 20),
        name="long_conv",
    )(recv.reshape((half, 2) + recv.shape[1:]), own_weight, end_terms(owned))
    return out.reshape(blocks, owned, LANES)


def local_streams(streams, tail, short_weight):
    taps = short_weight.shape[0]
    length = streams.shape[2]
    padded = jnp.concatenate([tail, streams], axis=2).astype(f32)
    conv = jnp.zeros(streams.shape, f32)
    for offset in range(taps):
        start = taps - 1 - offset
        conv = conv + short_weight[offset][:, :, None] * padded[:, :, start : start + length]
    return lax.optimization_barrier((conv[0].astype(bf16), (conv[1] * conv[2]).astype(bf16)))


def in_vmem(*arrays):
    return tuple(pltpu.with_memory_space_constraint(x, pltpu.VMEM) for x in arrays)


def gate(back, query, direct, gain):
    chan, length = query.shape
    chunk = chan // 4

    def kernel(back_ref, query_ref, direct_ref, gain_ref, out_ref, sum_ref):
        total = jnp.zeros((8, length), f32)
        for first in range(0, chan, chunk):
            rows = slice(first, first + chunk)
            mixed = back_ref[rows, :].astype(f32) + direct_ref[rows, :]
            gated = (query_ref[rows, :].astype(f32) * mixed).astype(bf16).astype(f32)
            out_ref[rows, :] = gated * gain_ref[rows, :]
            total = total + jnp.sum((gated * gated).reshape(chunk // 8, 8, length), axis=0)
        sum_ref[...] = jnp.sum(total, axis=0, keepdims=True)

    whole = pl.BlockSpec(memory_space=pltpu.VMEM)
    return pl.pallas_call(
        kernel,
        out_shape=(pltpu.VMEM((chan, length), f32), pltpu.VMEM((1, length), f32)),
        in_specs=[whole] * 4,
        out_specs=(whole, whole),
        compiler_params=pltpu.CompilerParams(vmem_limit_bytes=16 << 20),
        name="gate",
    )(*in_vmem(back, query, direct, gain))


def finish(gated, squares, count):
    chan, length = gated.shape

    parts = 4
    chunk = chan // parts

    def kernel(gated_ref, squares_ref, out_ref, done_ref, sems):
        scale = 1.0 / jnp.sqrt(jnp.sum(squares_ref[...], axis=0) / count + 1e-05)
        copies = []
        for part in range(parts):
            rows = pl.ds(part * chunk, chunk)
            done_ref[rows, :] = (gated_ref[rows, :] * scale).astype(bf16)
            copies.append(pltpu.make_async_copy(done_ref.at[rows], out_ref.at[rows], sems.at[part]))
            copies[part].start()
        for copy in copies:
            copy.wait()

    whole = pl.BlockSpec(memory_space=pltpu.VMEM)
    return pl.pallas_call(
        kernel,
        out_shape=jax.ShapeDtypeStruct((chan, length), bf16),
        in_specs=[whole, whole],
        out_specs=pl.BlockSpec(memory_space=pltpu.HBM),
        scratch_shapes=[pltpu.VMEM((chan, length), bf16), pltpu.SemaphoreType.DMA((parts,))],
        compiler_params=pltpu.CompilerParams(vmem_limit_bytes=16 << 20),
        name="finish",
    )(*in_vmem(gated), squares)


def shards(streams, short_weight, filters, skip_gain, norm_gain):
    n_ctx = lax.axis_size("ctx")
    n_width = lax.axis_size("tp")
    length = streams.shape[2]
    local_chan = streams.shape[1]
    owned = local_chan // n_ctx
    taps = short_weight.shape[0]
    send = pack_product(streams, short_weight, filters, owned)
    recv = lax.all_to_all(send, "ctx", 0, 0)
    streams, short_weight, _ = lax.optimization_barrier((streams, short_weight, send))
    own_weight = lax.dynamic_slice_in_dim(short_weight, lax.axis_index("ctx") * owned, owned, 2)
    own_weight = jnp.transpose(own_weight[:, 1:], (1, 0, 2)).reshape(2 * taps, owned)
    own_weight = jnp.pad(jnp.tile(own_weight, (1, 2)), ((0, 8 - 2 * taps), (0, LANES - 2 * owned)))
    tail = lax.ppermute(streams[:, :, length - (taps - 1) :], "ctx", [(i, i + 1) for i in range(n_ctx - 1)])
    mixed = long_conv_blocks(recv, own_weight, owned)
    back = lax.all_to_all(mixed, "ctx", 0, 0).reshape(local_chan, length)
    streams, tail, short_weight, skip_gain, norm_gain, _ = lax.optimization_barrier(
        (streams, tail, short_weight, skip_gain, norm_gain, mixed)
    )
    query, product = local_streams(streams, tail, short_weight)
    gain = jnp.broadcast_to(norm_gain[:, None], (local_chan, length))
    gain, product = lax.optimization_barrier((gain, product))
    direct = skip_gain[:, None] * product.astype(f32)
    direct, gain, query, back = lax.optimization_barrier((direct, gain, query, back))
    gated, squares = gate(back, query, direct, gain)
    return finish(gated, lax.all_gather(squares, "tp"), local_chan * n_width)


def solution(mesh):
    in_specs = (P(None, "tp", "ctx"), P(None, None, "tp"), P("tp", "ctx"), P("tp"), P("tp"))
    out_specs = P("tp", "ctx")
    return jax.shard_map(shards, mesh=mesh, in_specs=in_specs, out_specs=out_specs, check_vma=False)
```

```python
import jax
import jax.numpy as jnp
import numpy as np
from jax import lax
from jax.experimental import pallas as pl
from jax.experimental.pallas import tpu as pltpu
from jax.sharding import PartitionSpec as P

bf16 = jnp.bfloat16
f32 = jnp.float32
LANES = 128


def lane_iota(shape):
    return lax.broadcasted_iota(jnp.int32, shape, len(shape) - 1)


def row_iota(shape):
    return lax.broadcasted_iota(jnp.int32, shape, len(shape) - 2)


ENDS = (0, 1, LANES - 2, LANES - 1)


def pack_product(streams, short_weight, filters, owned):
    taps, _, chan = short_weight.shape
    owners = chan // owned
    parts = 2
    chunk = chan // parts
    per = chunk // owned
    terms = 2 * taps

    def kernel(streams_in, weight_in, filt_in, out_ref, raw_ref, weight_ref, filt_ref, pack_ref, sems, out_sems):
        weight_copy = pltpu.make_async_copy(weight_in, weight_ref, sems.at[0])
        raw_copy = pltpu.make_async_copy(streams_in.at[pl.ds(1, 2)], raw_ref, sems.at[1])
        filt_copy = pltpu.make_async_copy(filt_in, filt_ref, sems.at[2])
        weight_copy.start()
        raw_copy.start()
        filt_copy.start()
        src = row_iota((LANES, LANES))
        place = lane_iota((LANES, LANES)) // owned
        pick = []
        for stream in range(2):
            hit = jnp.zeros((LANES, LANES), f32)
            for n, pos in enumerate(ENDS):
                hit = jnp.where((place == 4 * stream + n) & (src == pos), 1.0, hit)
            pick.append(hit)
        pick = jnp.concatenate(pick, axis=0).astype(bf16)
        row = row_iota((32, terms * LANES))
        block = lane_iota((32, terms * LANES)) // LANES
        wanted = 3 * (block % taps) + block // taps + 1
        choose = jnp.where((row % (3 * taps) == wanted) & (row < 9 * taps), 1.0, 0.0).astype(bf16)
        shape = (chunk, LANES)
        inner = lane_iota(shape) >= taps - 1
        same = lane_iota(shape) % owned == row_iota(shape) % owned
        weight_copy.wait()
        weight = 0.5 * weight_ref[...].reshape(3 * taps, chan)
        high = weight.astype(bf16).astype(f32)
        middle = (weight - high).astype(bf16).astype(f32)
        split = [high, middle, weight - high - middle, jnp.zeros((32 - 9 * taps, chan), f32)]
        split = jnp.transpose(jnp.concatenate(split, axis=0)).astype(bf16)
        raw_copy.wait()
        filt_copy.wait()
        copies = []
        for part in range(parts):
            rows = slice(part * chunk, (part + 1) * chunk)
            own = slice(part * per, (part + 1) * per)
            along = jnp.dot(split[rows], choose, preferred_element_type=f32)
            convs = []
            for stream in range(2):
                raw = raw_ref[stream, rows]
                total = along[:, stream * taps * LANES : (stream * taps + 1) * LANES] * raw.astype(f32)
                for j in range(1, taps):
                    at = (stream * taps + j) * LANES
                    total = total + along[:, at : at + LANES] * pltpu.roll(raw, j, 1).astype(f32)
                convs.append(total + total)
            product = jnp.where(inner, convs[0] * convs[1], 0.0).astype(bf16)
            pack_ref[own, 0 : owned // 2] = product.reshape(per, owned // 2, 2, LANES)
            both = jnp.concatenate([raw_ref[0, rows], raw_ref[1, rows]], axis=1)
            spread = jnp.where(same, jnp.dot(both, pick, preferred_element_type=f32), 0.0)
            ends = jnp.sum(spread.reshape(per, owned, LANES), axis=1)
            first = row_iota((per, 2, LANES)) == 0
            rest = jnp.where(first, filt_ref[own][:, None, :], ends[:, None, :])
            pack_ref[own, owned // 2] = rest.astype(bf16)
            where = pl.ds(part * per, per)
            copies.append(pltpu.make_async_copy(pack_ref.at[where], out_ref.at[where], out_sems.at[part]))
            copies[part].start()
        for copy in copies:
            copy.wait()

    hbm = pl.BlockSpec(memory_space=pltpu.HBM)
    packed = (owners, owned // 2 + 1, 2, LANES)
    return pl.pallas_call(
        kernel,
        out_shape=jax.ShapeDtypeStruct(packed, bf16),
        in_specs=[hbm, hbm, hbm],
        out_specs=hbm,
        scratch_shapes=[
            pltpu.VMEM((2, chan, LANES), bf16),
            pltpu.VMEM((taps, 3, chan), f32),
            pltpu.VMEM((owners, LANES), f32),
            pltpu.VMEM(packed, bf16),
            pltpu.SemaphoreType.DMA((3,)),
            pltpu.SemaphoreType.DMA((parts,)),
        ],
        compiler_params=pltpu.CompilerParams(vmem_limit_bytes=32 << 20),
        name="pack_product",
    )(*(pltpu.with_memory_space_constraint(x, pltpu.HBM) for x in (streams, short_weight, filters)))


def end_terms(owned):
    pick = np.zeros((2 * LANES, 6 * LANES), np.float32)
    for stream in range(2):
        base = 4 * stream
        for n, sources in enumerate((((0, 0), (1, 0)), ((3, 1), (0, 0)), ((2, 1), (3, 1)))):
            for pos, (end, before) in enumerate(sources):
                for c in range(owned):
                    row = before * LANES + (base + end) * owned + c
                    pick[row, (3 * stream + n) * LANES + pos * owned + c] = 1.0
    return jnp.asarray(pick, bf16)


def long_conv_blocks(recv, own_weight, owned):
    blocks = recv.shape[0]
    half = blocks // 2
    rows = half * owned
    span = 2
    wide = 2 * LANES
    chunk = 256

    def kernel(recv_ref, weight_ref, terms_ref, out_ref, toep_ref, cols_ref, acc_ref, ends_ref, first_ref):
        for k in range(blocks):
            ends_ref[k : k + 1, :] = recv_ref[k // 2, k % 2, owned // 2].astype(f32)[1:2]
        ends = ends_ref[...]
        before = jnp.where(row_iota(ends.shape) == 0, 0.0, pltpu.roll(ends, 1, 0))
        both = jnp.concatenate([ends, before], axis=1).astype(bf16)
        terms = jnp.dot(both, terms_ref[...], preferred_element_type=f32)
        convs = []
        for stream in range(2):
            total = jnp.zeros((blocks, LANES), f32)
            for n in range(3):
                at = 3 * stream + n
                total = total + weight_ref[at : at + 1, :] * terms[:, at * LANES : (at + 1) * LANES]
            convs.append(total)
        first_ref[...] = (convs[0] * convs[1]).astype(bf16).astype(f32)
        shape = (owned, LANES)
        same = lane_iota(shape) % owned == row_iota(shape)
        src = row_iota((LANES, LANES))
        dst = lane_iota((LANES, LANES))
        to_lane = jnp.where((src // owned == dst) & (dst < 2), 1.0, 0.0).astype(bf16)
        for lag in range(1, span):
            cols_ref[0 : lag * owned, lag * wide : (lag + 1) * wide] = jnp.zeros((lag * owned, wide), bf16)
        for parity in range(2):
            for begin in range(0, rows, chunk):
                spread = []
                for pair in range(begin // owned, (begin + chunk) // owned):
                    block = 2 * pair + parity
                    values = jnp.broadcast_to(first_ref[block : block + 1, :], shape)
                    spread.append(jnp.where(same, values, 0.0))
                spread = jnp.concatenate(spread, axis=0).astype(bf16)
                patch = jnp.dot(spread, to_lane, preferred_element_type=f32)
                part = recv_ref[begin // owned : (begin + chunk) // owned, parity, 0 : owned // 2]
                part = (part.reshape(chunk, LANES).astype(f32) + patch).astype(bf16)
                for lag in range(span):
                    top = begin + lag * owned
                    size = min(chunk, rows - top)
                    left = lag * wide + parity * LANES
                    cols_ref[top : top + size, left : left + LANES] = part[0:size]
        upper = dst >= src
        toep_ref[0] = jnp.zeros((LANES, LANES), bf16)

        def build(first, count, before):
            for k in range(first, first + count):
                taps = recv_ref[k // 2, k % 2, owned // 2].astype(f32)[0:1]
                turned = pltpu.roll(jnp.broadcast_to(taps, (LANES, LANES)), 0, 1, stride=1, stride_axis=0)
                toep_ref[k + 1] = jnp.where(upper, turned, before).astype(bf16)
                before = turned
            return before

        before = build(0, 2 * span, jnp.zeros((LANES, LANES), f32))
        for step in range(half // span):
            if (step + 1) * span < half:
                before = build((step + 1) * 2 * span, 2 * span, before)
            parts = []
            for lag in range(step * span, (step + 1) * span):
                parts.append(jnp.concatenate([toep_ref[2 * lag + 1], toep_ref[2 * lag + 2]], axis=1))
                parts.append(jnp.concatenate([toep_ref[2 * lag], toep_ref[2 * lag + 1]], axis=1))
            start = step * span * owned
            added = jnp.dot(cols_ref[0 : rows - start, :], jnp.concatenate(parts, axis=0), preferred_element_type=f32)
            if step:
                acc_ref[start:rows, :] += added
            else:
                acc_ref[...] = added
        out_ref[:, 0] = acc_ref[:, 0:LANES].astype(bf16).reshape(half, owned, LANES)
        out_ref[:, 1] = acc_ref[:, LANES:wide].astype(bf16).reshape(half, owned, LANES)

    vmem = pl.BlockSpec(memory_space=pltpu.VMEM)
    out = pl.pallas_call(
        kernel,
        out_shape=jax.ShapeDtypeStruct((half, 2, owned, LANES), bf16),
        in_specs=[vmem, vmem, vmem],
        out_specs=vmem,
        scratch_shapes=[
            pltpu.VMEM((blocks + 1, LANES, LANES), bf16),
            pltpu.VMEM((rows, span * wide), bf16),
            pltpu.VMEM((rows, wide), f32),
            pltpu.VMEM((blocks, LANES), f32),
            pltpu.VMEM((blocks, LANES), f32),
        ],
        compiler_params=pltpu.CompilerParams(vmem_limit_bytes=32 << 20),
        name="long_conv",
    )(recv.reshape((half, 2) + recv.shape[1:]), own_weight, end_terms(owned))
    return out.reshape(blocks, owned, LANES)


def local_streams(streams, tail, short_weight):
    taps = short_weight.shape[0]
    length = streams.shape[2]
    padded = jnp.concatenate([tail, streams], axis=2).astype(f32)
    conv = jnp.zeros(streams.shape, f32)
    for offset in range(taps):
        start = taps - 1 - offset
        conv = conv + short_weight[offset][:, :, None] * padded[:, :, start : start + length]
    return lax.optimization_barrier((conv[0].astype(bf16), (conv[1] * conv[2]).astype(bf16)))


def in_vmem(*arrays):
    return tuple(pltpu.with_memory_space_constraint(x, pltpu.VMEM) for x in arrays)


def gate(back, query, direct, gain):
    chan, length = query.shape
    chunk = chan // 4

    def kernel(back_ref, query_ref, direct_ref, gain_ref, out_ref, sum_ref):
        total = jnp.zeros((8, length), f32)
        for first in range(0, chan, chunk):
            rows = slice(first, first + chunk)
            mixed = back_ref[rows, :].astype(f32) + direct_ref[rows, :]
            gated = (query_ref[rows, :].astype(f32) * mixed).astype(bf16).astype(f32)
            out_ref[rows, :] = gated * gain_ref[rows, :]
            total = total + jnp.sum((gated * gated).reshape(chunk // 8, 8, length), axis=0)
        sum_ref[...] = jnp.sum(total, axis=0, keepdims=True)

    whole = pl.BlockSpec(memory_space=pltpu.VMEM)
    return pl.pallas_call(
        kernel,
        out_shape=(pltpu.VMEM((chan, length), f32), pltpu.VMEM((1, length), f32)),
        in_specs=[whole] * 4,
        out_specs=(whole, whole),
        compiler_params=pltpu.CompilerParams(vmem_limit_bytes=16 << 20),
        name="gate",
    )(*in_vmem(back, query, direct, gain))


def finish(gated, squares, count):
    chan, length = gated.shape

    parts = 2
    chunk = chan // parts

    def kernel(gated_ref, squares_ref, out_ref, done_ref, sems):
        scale = 1.0 / jnp.sqrt(jnp.sum(squares_ref[...], axis=0) / count + 1e-05)
        copies = []
        for part in range(parts):
            rows = pl.ds(part * chunk, chunk)
            done_ref[rows, :] = (gated_ref[rows, :] * scale).astype(bf16)
            copies.append(pltpu.make_async_copy(done_ref.at[rows], out_ref.at[rows], sems.at[part]))
            copies[part].start()
        for copy in copies:
            copy.wait()

    whole = pl.BlockSpec(memory_space=pltpu.VMEM)
    return pl.pallas_call(
        kernel,
        out_shape=jax.ShapeDtypeStruct((chan, length), bf16),
        in_specs=[whole, whole],
        out_specs=pl.BlockSpec(memory_space=pltpu.HBM),
        scratch_shapes=[pltpu.VMEM((chan, length), bf16), pltpu.SemaphoreType.DMA((parts,))],
        compiler_params=pltpu.CompilerParams(vmem_limit_bytes=16 << 20),
        name="finish",
    )(*in_vmem(gated), squares)


def shards(streams, short_weight, filters, skip_gain, norm_gain):
    n_ctx = lax.axis_size("ctx")
    n_width = lax.axis_size("tp")
    length = streams.shape[2]
    local_chan = streams.shape[1]
    owned = local_chan // n_ctx
    taps = short_weight.shape[0]
    send = pack_product(streams, short_weight, filters, owned)
    recv = lax.all_to_all(send, "ctx", 0, 0)
    streams, short_weight, _ = lax.optimization_barrier((streams, short_weight, send))
    own_weight = lax.dynamic_slice_in_dim(short_weight, lax.axis_index("ctx") * owned, owned, 2)
    own_weight = jnp.transpose(own_weight[:, 1:], (1, 0, 2)).reshape(2 * taps, owned)
    own_weight = jnp.pad(jnp.tile(own_weight, (1, 2)), ((0, 8 - 2 * taps), (0, LANES - 2 * owned)))
    tail = lax.ppermute(streams[:, :, length - (taps - 1) :], "ctx", [(i, i + 1) for i in range(n_ctx - 1)])
    mixed = long_conv_blocks(recv, own_weight, owned)
    back = lax.all_to_all(mixed, "ctx", 0, 0).reshape(local_chan, length)
    streams, tail, short_weight, skip_gain, norm_gain, _ = lax.optimization_barrier(
        (streams, tail, short_weight, skip_gain, norm_gain, mixed)
    )
    query, product = local_streams(streams, tail, short_weight)
    gain = jnp.broadcast_to(norm_gain[:, None], (local_chan, length))
    gain, product = lax.optimization_barrier((gain, product))
    direct = skip_gain[:, None] * product.astype(f32)
    direct, gain, query, back = lax.optimization_barrier((direct, gain, query, back))
    gated, squares = gate(back, query, direct, gain)
    return finish(gated, lax.all_gather(squares, "tp"), local_chan * n_width)


def solution(mesh):
    in_specs = (P(None, "tp", "ctx"), P(None, None, "tp"), P("tp", "ctx"), P("tp"), P("tp"))
    out_specs = P("tp", "ctx")
    return jax.shard_map(shards, mesh=mesh, in_specs=in_specs, out_specs=out_specs, check_vma=False)
```

```python
import jax
import jax.numpy as jnp
import numpy as np
from jax import lax
from jax.experimental import pallas as pl
from jax.experimental.pallas import tpu as pltpu
from jax.sharding import PartitionSpec as P

bf16 = jnp.bfloat16
f32 = jnp.float32
LANES = 128


def lane_iota(shape):
    return lax.broadcasted_iota(jnp.int32, shape, len(shape) - 1)


def row_iota(shape):
    return lax.broadcasted_iota(jnp.int32, shape, len(shape) - 2)


ENDS = (0, 1, LANES - 2, LANES - 1)


def pack_product(streams, short_weight, filters, owned):
    taps, _, chan = short_weight.shape
    owners = chan // owned
    parts = 2
    chunk = chan // parts
    per = chunk // owned
    terms = 2 * taps

    def kernel(streams_in, weight_in, filt_in, out_ref, raw_ref, weight_ref, filt_ref, pack_ref, sems, out_sems):
        weight_copy = pltpu.make_async_copy(weight_in, weight_ref, sems.at[0])
        raw_copy = pltpu.make_async_copy(streams_in.at[pl.ds(1, 2)], raw_ref, sems.at[1])
        filt_copy = pltpu.make_async_copy(filt_in, filt_ref, sems.at[2])
        weight_copy.start()
        raw_copy.start()
        filt_copy.start()
        src = row_iota((LANES, LANES))
        place = lane_iota((LANES, LANES)) // owned
        pick = []
        for stream in range(2):
            hit = jnp.zeros((LANES, LANES), f32)
            for n, pos in enumerate(ENDS):
                hit = jnp.where((place == 4 * stream + n) & (src == pos), 1.0, hit)
            pick.append(hit)
        pick = jnp.concatenate(pick, axis=0).astype(bf16)
        row = row_iota((32, terms * LANES))
        block = lane_iota((32, terms * LANES)) // LANES
        wanted = 3 * (block % taps) + block // taps + 1
        choose = jnp.where((row % (3 * taps) == wanted) & (row < 9 * taps), 1.0, 0.0).astype(bf16)
        shape = (chunk, LANES)
        inner = lane_iota(shape) >= taps - 1
        same = lane_iota(shape) % owned == row_iota(shape) % owned
        weight_copy.wait()
        weight = 0.5 * weight_ref[...].reshape(3 * taps, chan)
        high = weight.astype(bf16).astype(f32)
        middle = (weight - high).astype(bf16).astype(f32)
        split = [high, middle, weight - high - middle, jnp.zeros((32 - 9 * taps, chan), f32)]
        split = jnp.transpose(jnp.concatenate(split, axis=0)).astype(bf16)
        raw_copy.wait()
        filt_copy.wait()
        copies = []
        for part in range(parts):
            rows = slice(part * chunk, (part + 1) * chunk)
            own = slice(part * per, (part + 1) * per)
            along = jnp.dot(split[rows], choose, preferred_element_type=f32)
            convs = []
            for stream in range(2):
                raw = raw_ref[stream, rows]
                total = along[:, stream * taps * LANES : (stream * taps + 1) * LANES] * raw.astype(f32)
                for j in range(1, taps):
                    at = (stream * taps + j) * LANES
                    total = total + along[:, at : at + LANES] * pltpu.roll(raw, j, 1).astype(f32)
                convs.append(total + total)
            product = jnp.where(inner, convs[0] * convs[1], 0.0).astype(bf16)
            pack_ref[own, 0 : owned // 2] = product.reshape(per, owned // 2, 2, LANES)
            both = jnp.concatenate([raw_ref[0, rows], raw_ref[1, rows]], axis=1)
            spread = jnp.where(same, jnp.dot(both, pick, preferred_element_type=f32), 0.0)
            ends = jnp.sum(spread.reshape(per, owned, LANES), axis=1)
            first = row_iota((per, 2, LANES)) == 0
            rest = jnp.where(first, filt_ref[own][:, None, :], ends[:, None, :])
            pack_ref[own, owned // 2] = rest.astype(bf16)
            where = pl.ds(part * per, per)
            copies.append(pltpu.make_async_copy(pack_ref.at[where], out_ref.at[where], out_sems.at[part]))
            copies[part].start()
        for copy in copies:
            copy.wait()

    hbm = pl.BlockSpec(memory_space=pltpu.HBM)
    packed = (owners, owned // 2 + 1, 2, LANES)
    return pl.pallas_call(
        kernel,
        out_shape=jax.ShapeDtypeStruct(packed, bf16),
        in_specs=[hbm, hbm, hbm],
        out_specs=hbm,
        scratch_shapes=[
            pltpu.VMEM((2, chan, LANES), bf16),
            pltpu.VMEM((taps, 3, chan), f32),
            pltpu.VMEM((owners, LANES), f32),
            pltpu.VMEM(packed, bf16),
            pltpu.SemaphoreType.DMA((3,)),
            pltpu.SemaphoreType.DMA((parts,)),
        ],
        compiler_params=pltpu.CompilerParams(vmem_limit_bytes=32 << 20),
        name="pack_product",
    )(*(pltpu.with_memory_space_constraint(x, pltpu.HBM) for x in (streams, short_weight, filters)))


def end_terms(owned):
    pick = np.zeros((2 * LANES, 6 * LANES), np.float32)
    for stream in range(2):
        base = 4 * stream
        for n, sources in enumerate((((0, 0), (1, 0)), ((3, 1), (0, 0)), ((2, 1), (3, 1)))):
            for pos, (end, before) in enumerate(sources):
                for c in range(owned):
                    row = before * LANES + (base + end) * owned + c
                    pick[row, (3 * stream + n) * LANES + pos * owned + c] = 1.0
    return jnp.asarray(pick, bf16)


def long_conv_blocks(recv, own_weight, owned):
    blocks = recv.shape[0]
    half = blocks // 2
    rows = half * owned
    wide = 2 * LANES
    chunk = 512

    def kernel(recv_ref, weight_ref, terms_ref, out_ref, toep_ref, cols_ref, acc_ref, ends_ref, first_ref):
        for k in range(blocks):
            ends_ref[k : k + 1, :] = recv_ref[k // 2, k % 2, owned // 2].astype(f32)[1:2]
        ends = ends_ref[...]
        before = jnp.where(row_iota(ends.shape) == 0, 0.0, pltpu.roll(ends, 1, 0))
        both = jnp.concatenate([ends, before], axis=1).astype(bf16)
        terms = jnp.dot(both, terms_ref[...], preferred_element_type=f32)
        convs = []
        for stream in range(2):
            total = jnp.zeros((blocks, LANES), f32)
            for n in range(3):
                at = 3 * stream + n
                total = total + weight_ref[at : at + 1, :] * terms[:, at * LANES : (at + 1) * LANES]
            convs.append(total)
        first_ref[...] = (convs[0] * convs[1]).astype(bf16).astype(f32)
        shape = (owned, LANES)
        same = lane_iota(shape) % owned == row_iota(shape)
        src = row_iota((LANES, LANES))
        dst = lane_iota((LANES, LANES))
        to_lane = jnp.where((src // owned == dst) & (dst < 2), 1.0, 0.0).astype(bf16)

        def place(begin):
            for parity in range(2):
                spread = []
                for pair in range(begin // owned, (begin + chunk) // owned):
                    block = 2 * pair + parity
                    values = jnp.broadcast_to(first_ref[block : block + 1, :], shape)
                    spread.append(jnp.where(same, values, 0.0))
                spread = jnp.concatenate(spread, axis=0).astype(bf16)
                patch = jnp.dot(spread, to_lane, preferred_element_type=f32)
                part = recv_ref[begin // owned : (begin + chunk) // owned, parity, 0 : owned // 2]
                part = (part.reshape(chunk, LANES).astype(f32) + patch).astype(bf16)
                cols_ref[begin : begin + chunk, parity * LANES : (parity + 1) * LANES] = part

        upper = dst >= src
        toep_ref[0] = jnp.zeros((LANES, LANES), bf16)

        def turn(k):
            taps = recv_ref[k // 2, k % 2, owned // 2].astype(f32)[0:1]
            return pltpu.roll(jnp.broadcast_to(taps, (LANES, LANES)), 0, 1, stride=1, stride_axis=0)

        def build(last, count, turned):
            for k in range(last, last - count, -1):
                before = turn(k - 1) if k else jnp.zeros((LANES, LANES), f32)
                toep_ref[k + 1] = jnp.where(upper, turned, before).astype(bf16)
                turned = before
            return turned

        turned = turn(blocks - 1)
        turned = build(blocks - 1, 3, turned)
        ready = 0
        for lag in reversed(range(half)):
            start = lag * owned
            while ready < rows - start:
                place(ready)
                ready += chunk
            if lag:
                turned = build(2 * lag - 2, 2 if lag > 1 else 1, turned)
            even = jnp.concatenate([toep_ref[2 * lag + 1], toep_ref[2 * lag + 2]], axis=1)
            odd = jnp.concatenate([toep_ref[2 * lag], toep_ref[2 * lag + 1]], axis=1)
            weights = jnp.concatenate([even, odd], axis=0)
            added = jnp.dot(cols_ref[0 : rows - start, :], weights, preferred_element_type=f32)
            acc_ref[start : start + owned, :] = added[0:owned]
            if lag + 1 < half:
                acc_ref[start + owned : rows, :] += added[owned:]
        out_ref[:, 0] = acc_ref[:, 0:LANES].astype(bf16).reshape(half, owned, LANES)
        out_ref[:, 1] = acc_ref[:, LANES:wide].astype(bf16).reshape(half, owned, LANES)

    vmem = pl.BlockSpec(memory_space=pltpu.VMEM)
    out = pl.pallas_call(
        kernel,
        out_shape=jax.ShapeDtypeStruct((half, 2, owned, LANES), bf16),
        in_specs=[vmem, vmem, vmem],
        out_specs=vmem,
        scratch_shapes=[
            pltpu.VMEM((blocks + 1, LANES, LANES), bf16),
            pltpu.VMEM((rows, wide), bf16),
            pltpu.VMEM((rows, wide), f32),
            pltpu.VMEM((blocks, LANES), f32),
            pltpu.VMEM((blocks, LANES), f32),
        ],
        compiler_params=pltpu.CompilerParams(vmem_limit_bytes=32 << 20),
        name="long_conv",
    )(recv.reshape((half, 2) + recv.shape[1:]), own_weight, end_terms(owned))
    return out.reshape(blocks, owned, LANES)


def local_streams(streams, tail, short_weight):
    taps = short_weight.shape[0]
    length = streams.shape[2]
    padded = jnp.concatenate([tail, streams], axis=2).astype(f32)
    conv = jnp.zeros(streams.shape, f32)
    for offset in range(taps):
        start = taps - 1 - offset
        conv = conv + short_weight[offset][:, :, None] * padded[:, :, start : start + length]
    return lax.optimization_barrier((conv[0].astype(bf16), (conv[1] * conv[2]).astype(bf16)))


def in_vmem(*arrays):
    return tuple(pltpu.with_memory_space_constraint(x, pltpu.VMEM) for x in arrays)


def gate(back, query, direct, gain):
    chan, length = query.shape
    chunk = chan // 4

    def kernel(back_ref, query_ref, direct_ref, gain_ref, out_ref, sum_ref):
        total = jnp.zeros((8, length), f32)
        for first in range(0, chan, chunk):
            rows = slice(first, first + chunk)
            mixed = back_ref[rows, :].astype(f32) + direct_ref[rows, :]
            gated = (query_ref[rows, :].astype(f32) * mixed).astype(bf16).astype(f32)
            out_ref[rows, :] = gated * gain_ref[rows, :]
            total = total + jnp.sum((gated * gated).reshape(chunk // 8, 8, length), axis=0)
        sum_ref[...] = jnp.sum(total, axis=0, keepdims=True)

    whole = pl.BlockSpec(memory_space=pltpu.VMEM)
    return pl.pallas_call(
        kernel,
        out_shape=(pltpu.VMEM((chan, length), f32), pltpu.VMEM((1, length), f32)),
        in_specs=[whole] * 4,
        out_specs=(whole, whole),
        compiler_params=pltpu.CompilerParams(vmem_limit_bytes=16 << 20),
        name="gate",
    )(*in_vmem(back, query, direct, gain))


def finish(gated, squares, count):
    chan, length = gated.shape

    parts = 2
    chunk = chan // parts

    def kernel(gated_ref, squares_ref, out_ref, done_ref, sems):
        scale = 1.0 / jnp.sqrt(jnp.sum(squares_ref[...], axis=0) / count + 1e-05)
        copies = []
        for part in range(parts):
            rows = pl.ds(part * chunk, chunk)
            done_ref[rows, :] = (gated_ref[rows, :] * scale).astype(bf16)
            copies.append(pltpu.make_async_copy(done_ref.at[rows], out_ref.at[rows], sems.at[part]))
            copies[part].start()
        for copy in copies:
            copy.wait()

    whole = pl.BlockSpec(memory_space=pltpu.VMEM)
    return pl.pallas_call(
        kernel,
        out_shape=jax.ShapeDtypeStruct((chan, length), bf16),
        in_specs=[whole, whole],
        out_specs=pl.BlockSpec(memory_space=pltpu.HBM),
        scratch_shapes=[pltpu.VMEM((chan, length), bf16), pltpu.SemaphoreType.DMA((parts,))],
        compiler_params=pltpu.CompilerParams(vmem_limit_bytes=16 << 20),
        name="finish",
    )(*in_vmem(gated), squares)


def shards(streams, short_weight, filters, skip_gain, norm_gain):
    n_ctx = lax.axis_size("ctx")
    n_width = lax.axis_size("tp")
    length = streams.shape[2]
    local_chan = streams.shape[1]
    owned = local_chan // n_ctx
    taps = short_weight.shape[0]
    send = pack_product(streams, short_weight, filters, owned)
    recv = lax.all_to_all(send, "ctx", 0, 0)
    streams, short_weight, _ = lax.optimization_barrier((streams, short_weight, send))
    own_weight = lax.dynamic_slice_in_dim(short_weight, lax.axis_index("ctx") * owned, owned, 2)
    own_weight = jnp.transpose(own_weight[:, 1:], (1, 0, 2)).reshape(2 * taps, owned)
    own_weight = jnp.pad(jnp.tile(own_weight, (1, 2)), ((0, 8 - 2 * taps), (0, LANES - 2 * owned)))
    tail = lax.ppermute(streams[:, :, length - (taps - 1) :], "ctx", [(i, i + 1) for i in range(n_ctx - 1)])
    mixed = long_conv_blocks(recv, own_weight, owned)
    back = lax.all_to_all(mixed, "ctx", 0, 0).reshape(local_chan, length)
    streams, tail, short_weight, skip_gain, norm_gain, _ = lax.optimization_barrier(
        (streams, tail, short_weight, skip_gain, norm_gain, mixed)
    )
    query, product = local_streams(streams, tail, short_weight)
    gain = jnp.broadcast_to(norm_gain[:, None], (local_chan, length))
    gain, product = lax.optimization_barrier((gain, product))
    direct = skip_gain[:, None] * product.astype(f32)
    direct, gain, query, back = lax.optimization_barrier((direct, gain, query, back))
    gated, squares = gate(back, query, direct, gain)
    return finish(gated, lax.all_gather(squares, "tp"), local_chan * n_width)


def solution(mesh):
    in_specs = (P(None, "tp", "ctx"), P(None, None, "tp"), P("tp", "ctx"), P("tp"), P("tp"))
    out_specs = P("tp", "ctx")
    return jax.shard_map(shards, mesh=mesh, in_specs=in_specs, out_specs=out_specs, check_vma=False)
```

```python
import jax
import jax.numpy as jnp
import numpy as np
from jax import lax
from jax.experimental import pallas as pl
from jax.experimental.pallas import tpu as pltpu
from jax.sharding import PartitionSpec as P

bf16 = jnp.bfloat16
f32 = jnp.float32
LANES = 128


def lane_iota(shape):
    return lax.broadcasted_iota(jnp.int32, shape, len(shape) - 1)


def row_iota(shape):
    return lax.broadcasted_iota(jnp.int32, shape, len(shape) - 2)


ENDS = (0, 1, LANES - 2, LANES - 1)


def pack_product(streams, short_weight, filters, owned):
    taps, _, chan = short_weight.shape
    owners = chan // owned
    parts = 2
    chunk = chan // parts
    per = chunk // owned
    terms = 2 * taps

    def kernel(streams_in, weight_in, filt_in, out_ref, raw_ref, weight_ref, filt_ref, pack_ref, sems, out_sems):
        weight_copy = pltpu.make_async_copy(weight_in, weight_ref, sems.at[0])
        raw_copy = pltpu.make_async_copy(streams_in.at[pl.ds(1, 2)], raw_ref, sems.at[1])
        filt_copy = pltpu.make_async_copy(filt_in, filt_ref, sems.at[2])
        weight_copy.start()
        raw_copy.start()
        filt_copy.start()
        src = row_iota((LANES, LANES))
        place = lane_iota((LANES, LANES)) // owned
        pick = []
        for stream in range(2):
            hit = jnp.zeros((LANES, LANES), f32)
            for n, pos in enumerate(ENDS):
                hit = jnp.where((place == 4 * stream + n) & (src == pos), 1.0, hit)
            pick.append(hit)
        pick = jnp.concatenate(pick, axis=0).astype(bf16)
        row = row_iota((32, terms * LANES))
        block = lane_iota((32, terms * LANES)) // LANES
        wanted = 3 * (block % taps) + block // taps + 1
        choose = jnp.where((row % (3 * taps) == wanted) & (row < 9 * taps), 1.0, 0.0).astype(bf16)
        shape = (chunk, LANES)
        inner = lane_iota(shape) >= taps - 1
        same = lane_iota(shape) % owned == row_iota(shape) % owned
        weight_copy.wait()
        weight = 0.5 * weight_ref[...].reshape(3 * taps, chan)
        high = weight.astype(bf16).astype(f32)
        middle = (weight - high).astype(bf16).astype(f32)
        split = [high, middle, weight - high - middle, jnp.zeros((32 - 9 * taps, chan), f32)]
        split = jnp.transpose(jnp.concatenate(split, axis=0)).astype(bf16)
        raw_copy.wait()
        filt_copy.wait()
        copies = []
        for part in range(parts):
            rows = slice(part * chunk, (part + 1) * chunk)
            own = slice(part * per, (part + 1) * per)
            along = jnp.dot(split[rows], choose, preferred_element_type=f32)
            convs = []
            for stream in range(2):
                raw = raw_ref[stream, rows]
                total = along[:, stream * taps * LANES : (stream * taps + 1) * LANES] * raw.astype(f32)
                for j in range(1, taps):
                    at = (stream * taps + j) * LANES
                    total = total + along[:, at : at + LANES] * pltpu.roll(raw, j, 1).astype(f32)
                convs.append(total + total)
            product = jnp.where(inner, convs[0] * convs[1], 0.0).astype(bf16)
            pack_ref[own, 0 : owned // 2] = product.reshape(per, owned // 2, 2, LANES)
            both = jnp.concatenate([raw_ref[0, rows], raw_ref[1, rows]], axis=1)
            spread = jnp.where(same, jnp.dot(both, pick, preferred_element_type=f32), 0.0)
            ends = jnp.sum(spread.reshape(per, owned, LANES), axis=1)
            first = row_iota((per, 2, LANES)) == 0
            rest = jnp.where(first, filt_ref[own][:, None, :], ends[:, None, :])
            pack_ref[own, owned // 2] = rest.astype(bf16)
            where = pl.ds(part * per, per)
            copies.append(pltpu.make_async_copy(pack_ref.at[where], out_ref.at[where], out_sems.at[part]))
            copies[part].start()
        for copy in copies:
            copy.wait()

    hbm = pl.BlockSpec(memory_space=pltpu.HBM)
    packed = (owners, owned // 2 + 1, 2, LANES)
    return pl.pallas_call(
        kernel,
        out_shape=jax.ShapeDtypeStruct(packed, bf16),
        in_specs=[hbm, hbm, hbm],
        out_specs=hbm,
        scratch_shapes=[
            pltpu.VMEM((2, chan, LANES), bf16),
            pltpu.VMEM((taps, 3, chan), f32),
            pltpu.VMEM((owners, LANES), f32),
            pltpu.VMEM(packed, bf16),
            pltpu.SemaphoreType.DMA((3,)),
            pltpu.SemaphoreType.DMA((parts,)),
        ],
        compiler_params=pltpu.CompilerParams(vmem_limit_bytes=32 << 20),
        name="pack_product",
    )(*(pltpu.with_memory_space_constraint(x, pltpu.HBM) for x in (streams, short_weight, filters)))


def end_terms(owned):
    pick = np.zeros((2 * LANES, 6 * LANES), np.float32)
    for stream in range(2):
        base = 4 * stream
        for n, sources in enumerate((((0, 0), (1, 0)), ((3, 1), (0, 0)), ((2, 1), (3, 1)))):
            for pos, (end, before) in enumerate(sources):
                for c in range(owned):
                    row = before * LANES + (base + end) * owned + c
                    pick[row, (3 * stream + n) * LANES + pos * owned + c] = 1.0
    return jnp.asarray(pick, bf16)


def long_conv_blocks(recv, own_weight, owned):
    blocks = recv.shape[0]
    half = blocks // 2
    rows = half * owned
    wide = 2 * LANES
    chunk = 512

    def kernel(recv_ref, weight_ref, terms_ref, out_ref, toep_ref, cols_ref, acc_ref, ends_ref, first_ref):
        for k in range(blocks):
            ends_ref[k : k + 1, :] = recv_ref[k // 2, k % 2, owned // 2].astype(f32)[1:2]
        ends = ends_ref[...]
        before = jnp.where(row_iota(ends.shape) == 0, 0.0, pltpu.roll(ends, 1, 0))
        both = jnp.concatenate([ends, before], axis=1).astype(bf16)
        terms = jnp.dot(both, terms_ref[...], preferred_element_type=f32)
        convs = []
        for stream in range(2):
            total = jnp.zeros((blocks, LANES), f32)
            for n in range(3):
                at = 3 * stream + n
                total = total + weight_ref[at : at + 1, :] * terms[:, at * LANES : (at + 1) * LANES]
            convs.append(total)
        first_ref[...] = (convs[0] * convs[1]).astype(bf16).astype(f32)
        shape = (owned, LANES)
        same = lane_iota(shape) % owned == row_iota(shape)
        src = row_iota((LANES, LANES))
        dst = lane_iota((LANES, LANES))
        to_lane = jnp.where((src // owned == dst) & (dst < 2), 1.0, 0.0).astype(bf16)

        def place(begin):
            for parity in range(2):
                spread = []
                for pair in range(begin // owned, (begin + chunk) // owned):
                    block = 2 * pair + parity
                    values = jnp.broadcast_to(first_ref[block : block + 1, :], shape)
                    spread.append(jnp.where(same, values, 0.0))
                spread = jnp.concatenate(spread, axis=0).astype(bf16)
                patch = jnp.dot(spread, to_lane, preferred_element_type=f32)
                part = recv_ref[begin // owned : (begin + chunk) // owned, parity, 0 : owned // 2]
                part = (part.reshape(chunk, LANES).astype(f32) + patch).astype(bf16)
                cols_ref[begin : begin + chunk, parity * LANES : (parity + 1) * LANES] = part

        upper = dst >= src
        toep_ref[0] = jnp.zeros((LANES, LANES), bf16)

        def turn(k):
            taps = recv_ref[k // 2, k % 2, owned // 2].astype(f32)[0:1]
            return pltpu.roll(jnp.broadcast_to(taps, (LANES, LANES)), 0, 1, stride=1, stride_axis=0)

        def build(last, count, turned):
            for k in range(last, last - count, -1):
                before = turn(k - 1) if k else jnp.zeros((LANES, LANES), f32)
                toep_ref[k + 1] = jnp.where(upper, turned, before).astype(bf16)
                turned = before
            return turned

        turned = turn(blocks - 1)
        turned = build(blocks - 1, 3, turned)
        ready = 0
        for lag in reversed(range(half)):
            start = lag * owned
            while ready < rows - start:
                place(ready)
                ready += chunk
            if lag:
                turned = build(2 * lag - 2, 2 if lag > 1 else 1, turned)
            even = jnp.concatenate([toep_ref[2 * lag + 1], toep_ref[2 * lag + 2]], axis=1)
            odd = jnp.concatenate([toep_ref[2 * lag], toep_ref[2 * lag + 1]], axis=1)
            weights = jnp.concatenate([even, odd], axis=0)
            added = jnp.dot(cols_ref[0 : rows - start, :], weights, preferred_element_type=f32)
            acc_ref[start : start + owned, :] = added[0:owned]
            if lag + 1 < half:
                acc_ref[start + owned : rows, :] += added[owned:]
        out_ref[:, 0] = acc_ref[:, 0:LANES].astype(bf16).reshape(half, owned, LANES)
        out_ref[:, 1] = acc_ref[:, LANES:wide].astype(bf16).reshape(half, owned, LANES)

    vmem = pl.BlockSpec(memory_space=pltpu.VMEM)
    out = pl.pallas_call(
        kernel,
        out_shape=jax.ShapeDtypeStruct((half, 2, owned, LANES), bf16),
        in_specs=[vmem, vmem, vmem],
        out_specs=vmem,
        scratch_shapes=[
            pltpu.VMEM((blocks + 1, LANES, LANES), bf16),
            pltpu.VMEM((rows, wide), bf16),
            pltpu.VMEM((rows, wide), f32),
            pltpu.VMEM((blocks, LANES), f32),
            pltpu.VMEM((blocks, LANES), f32),
        ],
        compiler_params=pltpu.CompilerParams(vmem_limit_bytes=32 << 20),
        name="long_conv",
    )(recv.reshape((half, 2) + recv.shape[1:]), own_weight, end_terms(owned))
    return out.reshape(blocks, owned, LANES)


def local_streams(streams, tail, short_weight):
    taps = short_weight.shape[0]
    length = streams.shape[2]
    padded = jnp.concatenate([tail, streams], axis=2).astype(f32)
    conv = jnp.zeros(streams.shape, f32)
    for offset in range(taps):
        start = taps - 1 - offset
        conv = conv + short_weight[offset][:, :, None] * padded[:, :, start : start + length]
    return lax.optimization_barrier((conv[0].astype(bf16), (conv[1] * conv[2]).astype(bf16)))


def in_vmem(*arrays):
    return tuple(pltpu.with_memory_space_constraint(x, pltpu.VMEM) for x in arrays)


def gate(back, query, direct, gain, copies):
    chan, length = query.shape
    chunk = chan // 4

    def kernel(back_ref, query_ref, direct_ref, gain_ref, out_ref, sum_ref):
        total = jnp.zeros((8, length), f32)
        for first in range(0, chan, chunk):
            rows = slice(first, first + chunk)
            mixed = back_ref[rows, :].astype(f32) + direct_ref[rows, :]
            gated = (query_ref[rows, :].astype(f32) * mixed).astype(bf16).astype(f32)
            out_ref[rows, :] = gated * gain_ref[rows, :]
            total = total + jnp.sum((gated * gated).reshape(chunk // 8, 8, length), axis=0)
        sum_ref[...] = jnp.broadcast_to(jnp.sum(total, axis=0, keepdims=True), (copies, 1, length))

    whole = pl.BlockSpec(memory_space=pltpu.VMEM)
    return pl.pallas_call(
        kernel,
        out_shape=(pltpu.VMEM((chan, length), f32), pltpu.VMEM((copies, 1, length), f32)),
        in_specs=[whole] * 4,
        out_specs=(whole, whole),
        compiler_params=pltpu.CompilerParams(vmem_limit_bytes=16 << 20),
        name="gate",
    )(*in_vmem(back, query, direct, gain))


def finish(gated, squares, count):
    chan, length = gated.shape

    parts = 2
    chunk = chan // parts

    def kernel(gated_ref, squares_ref, out_ref, done_ref, sems):
        scale = 1.0 / jnp.sqrt(jnp.sum(squares_ref[...], axis=0) / count + 1e-05)
        copies = []
        for part in range(parts):
            rows = pl.ds(part * chunk, chunk)
            done_ref[rows, :] = (gated_ref[rows, :] * scale).astype(bf16)
            copies.append(pltpu.make_async_copy(done_ref.at[rows], out_ref.at[rows], sems.at[part]))
            copies[part].start()
        for copy in copies:
            copy.wait()

    whole = pl.BlockSpec(memory_space=pltpu.VMEM)
    return pl.pallas_call(
        kernel,
        out_shape=jax.ShapeDtypeStruct((chan, length), bf16),
        in_specs=[whole, whole],
        out_specs=pl.BlockSpec(memory_space=pltpu.HBM),
        scratch_shapes=[pltpu.VMEM((chan, length), bf16), pltpu.SemaphoreType.DMA((parts,))],
        compiler_params=pltpu.CompilerParams(vmem_limit_bytes=16 << 20),
        name="finish",
    )(*in_vmem(gated), squares)


def shards(streams, short_weight, filters, skip_gain, norm_gain):
    n_ctx = lax.axis_size("ctx")
    n_width = lax.axis_size("tp")
    length = streams.shape[2]
    local_chan = streams.shape[1]
    owned = local_chan // n_ctx
    taps = short_weight.shape[0]
    send = pack_product(streams, short_weight, filters, owned)
    recv = lax.all_to_all(send, "ctx", 0, 0)
    streams, short_weight, _ = lax.optimization_barrier((streams, short_weight, send))
    own_weight = lax.dynamic_slice_in_dim(short_weight, lax.axis_index("ctx") * owned, owned, 2)
    own_weight = jnp.transpose(own_weight[:, 1:], (1, 0, 2)).reshape(2 * taps, owned)
    own_weight = jnp.pad(jnp.tile(own_weight, (1, 2)), ((0, 8 - 2 * taps), (0, LANES - 2 * owned)))
    tail = lax.ppermute(streams[:, :, length - (taps - 1) :], "ctx", [(i, i + 1) for i in range(n_ctx - 1)])
    mixed = long_conv_blocks(recv, own_weight, owned)
    back = lax.all_to_all(mixed, "ctx", 0, 0).reshape(local_chan, length)
    streams, tail, short_weight, skip_gain, norm_gain, _ = lax.optimization_barrier(
        (streams, tail, short_weight, skip_gain, norm_gain, mixed)
    )
    query, product = local_streams(streams, tail, short_weight)
    gain = jnp.broadcast_to(norm_gain[:, None], (local_chan, length))
    gain, product = lax.optimization_barrier((gain, product))
    direct = skip_gain[:, None] * product.astype(f32)
    direct, gain, query, back = lax.optimization_barrier((direct, gain, query, back))
    gated, squares = gate(back, query, direct, gain, n_width)
    return finish(gated, lax.all_to_all(squares, "tp", 0, 0), local_chan * n_width)


def solution(mesh):
    in_specs = (P(None, "tp", "ctx"), P(None, None, "tp"), P("tp", "ctx"), P("tp"), P("tp"))
    out_specs = P("tp", "ctx")
    return jax.shard_map(shards, mesh=mesh, in_specs=in_specs, out_specs=out_specs, check_vma=False)
```

```python
import jax
import jax.numpy as jnp
import numpy as np
from jax import lax
from jax.experimental import pallas as pl
from jax.experimental.pallas import tpu as pltpu
from jax.sharding import PartitionSpec as P

bf16 = jnp.bfloat16
f32 = jnp.float32
LANES = 128


def lane_iota(shape):
    return lax.broadcasted_iota(jnp.int32, shape, len(shape) - 1)


def row_iota(shape):
    return lax.broadcasted_iota(jnp.int32, shape, len(shape) - 2)


ENDS = (0, 1, LANES - 2, LANES - 1)


def pack_product(streams, short_weight, filters, owned):
    taps, _, chan = short_weight.shape
    owners = chan // owned
    parts = 2
    chunk = chan // parts
    per = chunk // owned
    terms = 2 * taps

    def kernel(streams_in, weight_in, filt_in, out_ref, raw_ref, weight_ref, filt_ref, pack_ref, sems, out_sems):
        weight_copy = pltpu.make_async_copy(weight_in, weight_ref, sems.at[0])
        raw_copy = pltpu.make_async_copy(streams_in.at[pl.ds(1, 2)], raw_ref, sems.at[1])
        filt_copy = pltpu.make_async_copy(filt_in, filt_ref, sems.at[2])
        weight_copy.start()
        raw_copy.start()
        filt_copy.start()
        src = row_iota((LANES, LANES))
        place = lane_iota((LANES, LANES)) // owned
        pick = []
        for stream in range(2):
            hit = jnp.zeros((LANES, LANES), f32)
            for n, pos in enumerate(ENDS):
                hit = jnp.where((place == 4 * stream + n) & (src == pos), 1.0, hit)
            pick.append(hit)
        pick = jnp.concatenate(pick, axis=0).astype(bf16)
        row = row_iota((32, terms * LANES))
        block = lane_iota((32, terms * LANES)) // LANES
        wanted = 3 * (block % taps) + block // taps + 1
        choose = jnp.where((row % (3 * taps) == wanted) & (row < 9 * taps), 1.0, 0.0).astype(bf16)
        shape = (chunk, LANES)
        inner = lane_iota(shape) >= taps - 1
        same = lane_iota(shape) % owned == row_iota(shape) % owned
        weight_copy.wait()
        weight = 0.5 * weight_ref[...].reshape(3 * taps, chan)
        high = weight.astype(bf16).astype(f32)
        middle = (weight - high).astype(bf16).astype(f32)
        split = [high, middle, weight - high - middle, jnp.zeros((32 - 9 * taps, chan), f32)]
        split = jnp.transpose(jnp.concatenate(split, axis=0)).astype(bf16)
        raw_copy.wait()
        filt_copy.wait()
        copies = []
        for part in range(parts):
            rows = slice(part * chunk, (part + 1) * chunk)
            own = slice(part * per, (part + 1) * per)
            along = jnp.dot(split[rows], choose, preferred_element_type=f32)
            convs = []
            for stream in range(2):
                raw = raw_ref[stream, rows]
                total = along[:, stream * taps * LANES : (stream * taps + 1) * LANES] * raw.astype(f32)
                for j in range(1, taps):
                    at = (stream * taps + j) * LANES
                    total = total + along[:, at : at + LANES] * pltpu.roll(raw, j, 1).astype(f32)
                convs.append(total + total)
            product = jnp.where(inner, convs[0] * convs[1], 0.0).astype(bf16)
            pack_ref[own, 0 : owned // 2] = product.reshape(per, owned // 2, 2, LANES)
            both = jnp.concatenate([raw_ref[0, rows], raw_ref[1, rows]], axis=1)
            spread = jnp.where(same, jnp.dot(both, pick, preferred_element_type=f32), 0.0)
            ends = jnp.sum(spread.reshape(per, owned, LANES), axis=1)
            first = row_iota((per, 2, LANES)) == 0
            rest = jnp.where(first, filt_ref[own][:, None, :], ends[:, None, :])
            pack_ref[own, owned // 2] = rest.astype(bf16)
            where = pl.ds(part * per, per)
            copies.append(pltpu.make_async_copy(pack_ref.at[where], out_ref.at[where], out_sems.at[part]))
            copies[part].start()
        for copy in copies:
            copy.wait()

    hbm = pl.BlockSpec(memory_space=pltpu.HBM)
    packed = (owners, owned // 2 + 1, 2, LANES)
    return pl.pallas_call(
        kernel,
        out_shape=jax.ShapeDtypeStruct(packed, bf16),
        in_specs=[hbm, hbm, hbm],
        out_specs=hbm,
        scratch_shapes=[
            pltpu.VMEM((2, chan, LANES), bf16),
            pltpu.VMEM((taps, 3, chan), f32),
            pltpu.VMEM((owners, LANES), f32),
            pltpu.VMEM(packed, bf16),
            pltpu.SemaphoreType.DMA((3,)),
            pltpu.SemaphoreType.DMA((parts,)),
        ],
        compiler_params=pltpu.CompilerParams(vmem_limit_bytes=32 << 20),
        name="pack_product",
    )(*(pltpu.with_memory_space_constraint(x, pltpu.HBM) for x in (streams, short_weight, filters)))


def end_terms(owned):
    pick = np.zeros((2 * LANES, 6 * LANES), np.float32)
    for stream in range(2):
        base = 4 * stream
        for n, sources in enumerate((((0, 0), (1, 0)), ((3, 1), (0, 0)), ((2, 1), (3, 1)))):
            for pos, (end, before) in enumerate(sources):
                for c in range(owned):
                    row = before * LANES + (base + end) * owned + c
                    pick[row, (3 * stream + n) * LANES + pos * owned + c] = 1.0
    return jnp.asarray(pick, bf16)


def long_conv_blocks(recv, own_weight, owned):
    blocks = recv.shape[0]
    half = blocks // 2
    rows = half * owned
    wide = 2 * LANES
    chunk = 512

    def kernel(recv_ref, weight_ref, terms_ref, out_ref, toep_ref, cols_ref, acc_ref, ends_ref, first_ref):
        for k in range(blocks):
            ends_ref[k : k + 1, :] = recv_ref[k // 2, k % 2, owned // 2].astype(f32)[1:2]
        ends = ends_ref[...]
        before = jnp.where(row_iota(ends.shape) == 0, 0.0, pltpu.roll(ends, 1, 0))
        both = jnp.concatenate([ends, before], axis=1).astype(bf16)
        terms = jnp.dot(both, terms_ref[...], preferred_element_type=f32)
        convs = []
        for stream in range(2):
            total = jnp.zeros((blocks, LANES), f32)
            for n in range(3):
                at = 3 * stream + n
                total = total + weight_ref[at : at + 1, :] * terms[:, at * LANES : (at + 1) * LANES]
            convs.append(total)
        first_ref[...] = (convs[0] * convs[1]).astype(bf16).astype(f32)
        shape = (owned, LANES)
        same = lane_iota(shape) % owned == row_iota(shape)
        src = row_iota((LANES, LANES))
        dst = lane_iota((LANES, LANES))
        to_lane = jnp.where((src // owned == dst) & (dst < 2), 1.0, 0.0).astype(bf16)

        def place(begin):
            for parity in range(2):
                spread = []
                for pair in range(begin // owned, (begin + chunk) // owned):
                    block = 2 * pair + parity
                    values = jnp.broadcast_to(first_ref[block : block + 1, :], shape)
                    spread.append(jnp.where(same, values, 0.0))
                spread = jnp.concatenate(spread, axis=0).astype(bf16)
                patch = jnp.dot(spread, to_lane, preferred_element_type=f32)
                part = recv_ref[begin // owned : (begin + chunk) // owned, parity, 0 : owned // 2]
                part = (part.reshape(chunk, LANES).astype(f32) + patch).astype(bf16)
                cols_ref[begin : begin + chunk, parity * LANES : (parity + 1) * LANES] = part

        upper = dst >= src
        toep_ref[0] = jnp.zeros((LANES, LANES), bf16)

        def turn(k):
            taps = recv_ref[k // 2, k % 2, owned // 2].astype(f32)[0:1]
            return pltpu.roll(jnp.broadcast_to(taps, (LANES, LANES)), 0, 1, stride=1, stride_axis=0)

        def build(last, count, turned):
            for k in range(last, last - count, -1):
                before = turn(k - 1) if k else jnp.zeros((LANES, LANES), f32)
                toep_ref[k + 1] = jnp.where(upper, turned, before).astype(bf16)
                turned = before
            return turned

        turned = turn(blocks - 1)
        turned = build(blocks - 1, 3, turned)
        ready = 0
        for lag in reversed(range(half)):
            start = lag * owned
            while ready < rows - start:
                place(ready)
                ready += chunk
            if lag:
                turned = build(2 * lag - 2, 2 if lag > 1 else 1, turned)
            even = jnp.concatenate([toep_ref[2 * lag + 1], toep_ref[2 * lag + 2]], axis=1)
            odd = jnp.concatenate([toep_ref[2 * lag], toep_ref[2 * lag + 1]], axis=1)
            weights = jnp.concatenate([even, odd], axis=0)
            added = jnp.dot(cols_ref[0 : rows - start, :], weights, preferred_element_type=f32)
            acc_ref[start : start + owned, :] = added[0:owned]
            if lag + 1 < half:
                acc_ref[start + owned : rows, :] += added[owned:]
        out_ref[:, 0] = acc_ref[:, 0:LANES].astype(bf16).reshape(half, owned, LANES)
        out_ref[:, 1] = acc_ref[:, LANES:wide].astype(bf16).reshape(half, owned, LANES)

    vmem = pl.BlockSpec(memory_space=pltpu.VMEM)
    out = pl.pallas_call(
        kernel,
        out_shape=jax.ShapeDtypeStruct((half, 2, owned, LANES), bf16),
        in_specs=[vmem, vmem, vmem],
        out_specs=vmem,
        scratch_shapes=[
            pltpu.VMEM((blocks + 1, LANES, LANES), bf16),
            pltpu.VMEM((rows, wide), bf16),
            pltpu.VMEM((rows, wide), f32),
            pltpu.VMEM((blocks, LANES), f32),
            pltpu.VMEM((blocks, LANES), f32),
        ],
        compiler_params=pltpu.CompilerParams(vmem_limit_bytes=32 << 20),
        name="long_conv",
    )(recv.reshape((half, 2) + recv.shape[1:]), own_weight, end_terms(owned))
    return out.reshape(blocks, owned, LANES)


def local_streams(streams, tail, short_weight):
    taps = short_weight.shape[0]
    length = streams.shape[2]
    padded = jnp.concatenate([tail, streams], axis=2).astype(f32)
    conv = jnp.zeros(streams.shape, f32)
    for offset in range(taps):
        start = taps - 1 - offset
        conv = conv + short_weight[offset][:, :, None] * padded[:, :, start : start + length]
    return lax.optimization_barrier((conv[0].astype(bf16), (conv[1] * conv[2]).astype(bf16)))


def in_vmem(*arrays):
    return tuple(pltpu.with_memory_space_constraint(x, pltpu.VMEM) for x in arrays)


def gate(back, query, direct, gain):
    chan, length = query.shape
    chunk = chan // 4

    def kernel(back_ref, query_ref, direct_ref, gain_ref, out_ref, sum_ref):
        total = jnp.zeros((8, length), f32)
        for first in range(0, chan, chunk):
            rows = slice(first, first + chunk)
            mixed = back_ref[rows, :].astype(f32) + direct_ref[rows, :]
            gated = (query_ref[rows, :].astype(f32) * mixed).astype(bf16).astype(f32)
            out_ref[rows, :] = gated * gain_ref[rows, :]
            total = total + jnp.sum((gated * gated).reshape(chunk // 8, 8, length), axis=0)
        sum_ref[...] = jnp.sum(total, axis=0, keepdims=True)

    whole = pl.BlockSpec(memory_space=pltpu.VMEM)
    return pl.pallas_call(
        kernel,
        out_shape=(pltpu.VMEM((chan, length), f32), pltpu.VMEM((1, length), f32)),
        in_specs=[whole] * 4,
        out_specs=(whole, whole),
        compiler_params=pltpu.CompilerParams(vmem_limit_bytes=16 << 20),
        name="gate",
    )(*in_vmem(back, query, direct, gain))


def finish(gated, squares, count):
    chan, length = gated.shape

    parts = 1
    chunk = chan // parts

    def kernel(gated_ref, squares_ref, out_ref, done_ref, sems):
        scale = 1.0 / jnp.sqrt(jnp.sum(squares_ref[...], axis=0) / count + 1e-05)
        copies = []
        for part in range(parts):
            rows = pl.ds(part * chunk, chunk)
            done_ref[rows, :] = (gated_ref[rows, :] * scale).astype(bf16)
            copies.append(pltpu.make_async_copy(done_ref.at[rows], out_ref.at[rows], sems.at[part]))
            copies[part].start()
        for copy in copies:
            copy.wait()

    whole = pl.BlockSpec(memory_space=pltpu.VMEM)
    return pl.pallas_call(
        kernel,
        out_shape=jax.ShapeDtypeStruct((chan, length), bf16),
        in_specs=[whole, whole],
        out_specs=pl.BlockSpec(memory_space=pltpu.HBM),
        scratch_shapes=[pltpu.VMEM((chan, length), bf16), pltpu.SemaphoreType.DMA((parts,))],
        compiler_params=pltpu.CompilerParams(vmem_limit_bytes=16 << 20),
        name="finish",
    )(*in_vmem(gated), squares)


def shards(streams, short_weight, filters, skip_gain, norm_gain):
    n_ctx = lax.axis_size("ctx")
    n_width = lax.axis_size("tp")
    length = streams.shape[2]
    local_chan = streams.shape[1]
    owned = local_chan // n_ctx
    taps = short_weight.shape[0]
    send = pack_product(streams, short_weight, filters, owned)
    recv = lax.all_to_all(send, "ctx", 0, 0)
    streams, short_weight, _ = lax.optimization_barrier((streams, short_weight, send))
    own_weight = lax.dynamic_slice_in_dim(short_weight, lax.axis_index("ctx") * owned, owned, 2)
    own_weight = jnp.transpose(own_weight[:, 1:], (1, 0, 2)).reshape(2 * taps, owned)
    own_weight = jnp.pad(jnp.tile(own_weight, (1, 2)), ((0, 8 - 2 * taps), (0, LANES - 2 * owned)))
    tail = lax.ppermute(streams[:, :, length - (taps - 1) :], "ctx", [(i, i + 1) for i in range(n_ctx - 1)])
    mixed = long_conv_blocks(recv, own_weight, owned)
    back = lax.all_to_all(mixed, "ctx", 0, 0).reshape(local_chan, length)
    streams, tail, short_weight, skip_gain, norm_gain, _ = lax.optimization_barrier(
        (streams, tail, short_weight, skip_gain, norm_gain, mixed)
    )
    query, product = local_streams(streams, tail, short_weight)
    gain = jnp.broadcast_to(norm_gain[:, None], (local_chan, length))
    gain, product = lax.optimization_barrier((gain, product))
    direct = skip_gain[:, None] * product.astype(f32)
    direct, gain, query, back = lax.optimization_barrier((direct, gain, query, back))
    gated, squares = gate(back, query, direct, gain)
    return finish(gated, lax.all_gather(squares, "tp"), local_chan * n_width)


def solution(mesh):
    in_specs = (P(None, "tp", "ctx"), P(None, None, "tp"), P("tp", "ctx"), P("tp"), P("tp"))
    out_specs = P("tp", "ctx")
    return jax.shard_map(shards, mesh=mesh, in_specs=in_specs, out_specs=out_specs, check_vma=False)
```
